1024 devices in a mesh: tm: 256 (over y, z, core), col: 4 (over x).
Axes of the slice: x: 4, y: 8, z: 16, core: 2. Of those that a mesh axis runs over, the one named last changes fastest.
Arguments:
- design: bfloat16 [32768, 2, 1024], P('tm', None, 'col'), may hold values from -512 to 512
- filter_taps: bfloat16 [256, 2, 512], replicated, may hold values from -3 to 3
- segment: int32 [32768], P('tm'), may hold values from 0 to 255, never falling along the last dimension, each value on 1 to 256 neighbouring positions
- valid_flags: int32 [32768], P('tm'), may hold values 0 or 1
- weights: float32 [2, 32768], P(None, 'tm'), may hold values from 0.05 to 20
- block_ids: int32 [4], replicated, may hold values from 0 to 3, each once
Outputs:
- normals: float32 [1024, 1024], P('tm', 'col')
The draws below stay inside these ranges and needn't reach their ends.
All inputs are finite; a program needn't handle non-finite values. No bound on the sum of `valid_flags` on one device may be relied on, other than what follows from the above.
Results may differ from the reference program's by a relative error of at most 0.0013.
Values may be sent and summed in bfloat16 or wider, within the bound.
A program may use at most 32 MiB of HBM per device.

```python
import math
import jax
import jax.numpy as jnp
import numpy as np
from jax import lax

CB = 256
TAPS = 512
EP_DEV = 128
EPOCHS = 32768
COLS = 1024
SEGS = 256
HB = 4
N_TM = 256
N_COL = 4


def draw_design(key, part):
    key_noise = jax.random.fold_in(key, 11)
    key_pair = jax.random.fold_in(key, 12)
    columns_all = CB * N_COL
    stripe = columns_all // N_TM
    values = jax.random.truncated_normal(key_noise, -6.0, 6.0, (EPOCHS, 2, columns_all), jnp.float32)
    pairing = jax.random.permutation(key_pair, N_TM)
    epoch_block = jnp.arange(EPOCHS) // EP_DEV
    column_block = jnp.arange(columns_all) // stripe
    boosted = pairing[epoch_block][:, None] == column_block[None, :]
    values = values * jnp.where(boosted, 16.0, 1.0)[:, None, :]
    mixed = values + 0.6 * jnp.roll(values, 1, axis=2)
    return mixed.astype(jnp.bfloat16)


def draw_filter_taps(key, part):
    key_base = jax.random.fold_in(key, 21)
    key_scale = jax.random.fold_in(key, 22)
    base = jax.random.truncated_normal(key_base, -6.0, 6.0, (SEGS, 2, TAPS), jnp.float32)
    seg_scale = jnp.exp(jax.random.uniform(key_scale, (SEGS, 2, 1), jnp.float32, math.log(0.5), math.log(2.0)))
    return (base * seg_scale / math.sqrt(TAPS)).astype(jnp.bfloat16)


def plant(entries, key, smallest, largest):
    place = [jax.random.randint(jax.random.fold_in(key, axis), (), 0, length) for axis, length in enumerate(entries.shape)]
    main_axis = entries.shape.index(max(entries.shape))
    neighbour = place[:main_axis] + [(place[main_axis] + 1) % entries.shape[main_axis]] + place[main_axis + 1:]
    return entries.at[tuple(place)].set(smallest).at[tuple(neighbour)].set(largest)


def steps_of(key, shape, cuts, low, top_value):
    gain = 1.0
    for axis_at, shards_of in cuts:
        heights = jax.random.uniform(jax.random.fold_in(jax.random.fold_in(key, 6), axis_at), (shards_of,), jnp.float32, low / len(cuts), top_value / len(cuts))
        gain = gain * jnp.repeat(jnp.exp(heights), shape[axis_at] // shards_of).reshape((-1,) + (1,) * (len(shape) - 1 - axis_at))
    return gain


def length_profile(number_of, total, limit, skew):
    loads = [(1 << 20) // math.isqrt(standing ** skew) + 1 for standing in range(2, number_of + 1)]
    surplus, given = total - limit - (number_of - 1), [1] * (number_of - 1)
    while surplus > 0:
        candidates = [i for i in range(number_of - 1) if given[i] < limit]
        mass, remaining = sum([loads[i] for i in candidates]), surplus
        for i in candidates:
            extra = min(limit - given[i], max(1, remaining * loads[i] // mass), surplus)
            given[i] = given[i] + extra
            surplus = surplus - extra
    return np.array([limit] + given)


def uneven(key, amount, total, limit, lean):
    if amount == 2:
        one = jax.random.randint(key, (), max(1, total - limit), min(limit, total - 1) + 1)
        return jnp.stack([one, total - one])
    lengths = jnp.asarray(length_profile(amount, total, limit, lean), jnp.int32)
    twos = (amount - 1) // 2
    donor, sink = lengths[1:1 + 2 * twos:2], lengths[2:2 + 2 * twos:2]
    slack = jnp.minimum(donor - 1, limit - sink)
    passed = jax.random.randint(jax.random.fold_in(key, 1), (twos,), 0, 1 << 20) % (slack + 1)
    lengths = lengths.at[1:1 + 2 * twos:2].set(donor - passed).at[2:2 + 2 * twos:2].set(sink + passed)
    return lengths[jax.random.permutation(jax.random.fold_in(key, 2), amount)]


def setup_inputs(seed: int = 0) -> dict:
    splits = jax.random.split(jax.random.key(seed), 7)
    return {
        "design": draw_design(jax.random.fold_in(splits[6], 71), 0),
        "filter_taps": draw_filter_taps(jax.random.fold_in(splits[6], 71), 0),
        "segment": jnp.searchsorted(jnp.cumsum(uneven(splits[2], SEGS, EPOCHS, 2 * EP_DEV, 0)), jnp.arange(EPOCHS), side="right").astype(jnp.int32),
        "valid_flags": plant((jax.random.randint(splits[3], (EPOCHS,), 0, 4) < 3).astype(jnp.int32), jax.random.fold_in(splits[3], 1), 0, 1),
        "weights": jnp.clip(jnp.exp(math.log(20.0) - 5.9914645 * jax.random.uniform(splits[4], (2, EPOCHS), jnp.float32) ** steps_of(splits[4], (2, EPOCHS), ((1, 256),), -0.2, 0.2)), 0.05, 20.0),
        "block_ids": jax.random.permutation(splits[5], N_COL).astype(jnp.int32),
    }


def reference(design, filter_taps, segment, valid_flags, weights, block_ids):
    window_rows = (HB + 1) * EP_DEV
    inverse = jnp.argsort(block_ids).astype(jnp.int32)
    padded = jnp.concatenate([jnp.zeros((HB * EP_DEV, 2, COLS), jnp.bfloat16), design], axis=0)
    row_weight = weights * valid_flags.astype(jnp.float32)[None, :]
    out_index = jnp.arange(EP_DEV, dtype=jnp.int32)[:, None]
    in_index = jnp.arange(window_rows, dtype=jnp.int32)[None, :]
    lag_index = HB * EP_DEV + out_index - in_index
    inside = (lag_index >= 0) & (lag_index < TAPS)
    clipped = jnp.clip(lag_index, 0, TAPS - 1).astype(jnp.int32)

    def accumulate(running, block_index):
        first_row = (block_index * EP_DEV).astype(jnp.int32)
        stacked = lax.dynamic_slice_in_dim(padded, first_row, window_rows, 0).astype(jnp.float32)
        segs_here = lax.dynamic_slice_in_dim(segment, first_row, EP_DEV, 0)
        tap_rows = filter_taps[segs_here].astype(jnp.float32)
        gathered = jnp.take_along_axis(tap_rows, jnp.broadcast_to(clipped[:, None, :], (EP_DEV, 2, window_rows)), axis=2)
        toeplitz = jnp.where(inside[:, None, :], gathered, jnp.zeros_like(gathered))
        filtered = jnp.einsum("tks,skc->tkc", toeplitz, stacked, precision=lax.Precision.HIGHEST).astype(jnp.bfloat16)
        ordered = filtered.reshape(EP_DEV, 2, N_COL, CB)[:, :, inverse, :].reshape(EP_DEV, 2, COLS)
        weight_here = lax.dynamic_slice_in_dim(row_weight, first_row, EP_DEV, 1)
        scaled = (ordered.astype(jnp.float32) * weight_here.T[:, :, None]).astype(jnp.bfloat16)
        left = ordered.reshape(2 * EP_DEV, COLS).astype(jnp.float32)
        right = scaled.reshape(2 * EP_DEV, COLS).astype(jnp.float32)
        running = running + jnp.dot(left.T, right, precision=lax.Precision.HIGHEST)
        return running, None

    summed, _ = lax.scan(accumulate, jnp.zeros((COLS, COLS), jnp.float32), jnp.arange(EPOCHS // EP_DEV, dtype=jnp.int32))
    return summed / (2.0 * EPOCHS)
```

```python
import functools

import jax
import jax.numpy as jnp
from jax import lax
from jax.experimental import pallas as pl
from jax.experimental.pallas import tpu as pltpu
from jax.sharding import PartitionSpec as P

MESH = pl.DeviceIdType.MESH
NY, NZ, NX = 8, 16, 4
CHIPS = NY * NZ
EP = 128
CB = 256
HALF = 128
TAPS = 512
BLOCKS = 4
PARTS = 2
F32 = jnp.float32
BF16 = jnp.bfloat16


def kernel(
    rows_ref,
    tap_ref,
    weight_ref,
    ids_ref,
    out_ref,
    window,
    taps_all,
    weights_all,
    toeplitz,
    gathered_0,
    gathered_1,
    scaled,
    gram,
    up_slots,
    down_slots,
    y_slots,
    total,
    own_send,
    own_recv,
    halo_send,
    halo_recv,
    far_send,
    far_recv,
    side_send,
    side_recv,
    col_send,
    col_recv,
    q_send,
    q_recv,
    up_send,
    up_recv,
    down_send,
    down_recv,
    y_send,
    y_recv,
):
    tm = lax.axis_index("tm")
    x = lax.axis_index("col")
    h = lax.rem(tm, 2)
    chip = tm // 2
    z = lax.rem(chip, NZ)
    y = chip // NZ
    other = 1 - h
    y_core = lax.rem(y, 2)

    def dev(chip_at, core, x_at=x):
        return {"tm": chip_at * 2 + core, "col": x_at}

    def remote(src, dst, send_sem, recv_sem, device):
        return pltpu.make_async_remote_copy(
            src_ref=src, dst_ref=dst, send_sem=send_sem, recv_sem=recv_sem, device_id=device, device_id_type=MESH
        )

    next_chip = lax.rem(chip + 1, CHIPS)
    prev_chip = lax.rem(chip + CHIPS - 1, CHIPS)
    x_up, x_down = lax.rem(x + 1, NX), lax.rem(x + NX - 1, NX)
    z_up = y * NZ + lax.rem(z + 1, NZ)
    z_down = y * NZ + lax.rem(z + NZ - 1, NZ)

    barrier = pltpu.get_barrier_semaphore()

    def greet(device):
        pl.semaphore_signal(barrier, inc=1, device_id=device, device_id_type=MESH)

    greet(dev(chip, other))
    greet(dev(prev_chip, 0))
    greet(dev(prev_chip, 1))
    greet(dev(chip, h, x_up))
    greet(dev(chip, h, x_down))
    greet(dev(z_up, h))
    greet(dev(z_down, h))
    on_diagonal = h == y_core
    for source in range(NY):

        @pl.when(jnp.logical_not(jnp.logical_and(source == y, on_diagonal)))
        def _():
            greet(dev(source * NZ + z, y_core))

    pl.semaphore_wait(barrier, 15 - on_diagonal.astype(jnp.int32))

    sends = []
    gathered = (gathered_0, gathered_1)

    def start(copy):
        copy.start()
        sends.append(copy)

    own_rows = pl.ds(pl.multiple_of(2 * TAPS // 2 + EP * h, EP), EP)
    near_rows = pl.ds(pl.multiple_of(TAPS // 2 + EP * h, EP), EP)
    my_cols = pl.ds(pl.multiple_of(HALF * h, HALF), HALF)
    other_cols = pl.ds(pl.multiple_of(HALF * other, HALF), HALF)

    for k in range(2):
        for core in range(2):
            start(
                remote(
                    rows_ref.at[k, :, pl.ds(HALF * core, HALF)],
                    window.at[k, near_rows, :],
                    halo_send.at[k, core],
                    halo_recv.at[k, h],
                    dev(next_chip, core),
                )
            )
    start(remote(tap_ref, taps_all.at[h], side_send.at[0], side_recv.at[0], dev(chip, other)))
    start(remote(weight_ref, weights_all.at[h], side_send.at[1], side_recv.at[1], dev(chip, other)))
    for k in range(2):
        start(
            remote(
                rows_ref.at[k, :, other_cols],
                window.at[k, own_rows, :],
                own_send.at[k],
                own_recv.at[k],
                dev(chip, other),
            )
        )
    for k in range(2):
        window[k, own_rows, :] = rows_ref[k, :, my_cols]
    taps_all[h] = tap_ref[...]
    weights_all[h] = weight_ref[...]

    def arrived(dst, recv_sem):
        remote(dst, dst, own_send.at[0], recv_sem, dev(chip, other)).wait_recv()

    row_at = lax.broadcasted_iota(jnp.int32, (TAPS, TAPS), 0)
    col_at = lax.broadcasted_iota(jnp.int32, (TAPS, TAPS), 1)
    flip = (row_at + col_at == TAPS - 1).astype(F32).astype(BF16)
    first_row = jnp.where(chip == 0, TAPS, jnp.where(chip == 1, TAPS // 2, 0))
    lane = lax.broadcasted_iota(jnp.int32, (2 * EP, TAPS + 2 * EP), 1)

    def build(k):
        tap_rows = jnp.concatenate([taps_all[0, k], taps_all[1, k]], axis=0)
        flipped = jnp.dot(tap_rows, flip, preferred_element_type=F32)
        wide = jnp.concatenate([flipped, jnp.zeros((2 * EP, 2 * EP), F32)], axis=1)
        skewed = pltpu.roll(wide, 1, 1, stride=1, stride_axis=0)
        toeplitz[k] = jnp.where(lane >= first_row, skewed, 0.0).astype(BF16)

    other_tap = taps_all.at[other]
    arrived(other_tap, side_recv.at[0])
    arrived(weights_all.at[other], side_recv.at[1])
    build(0)
    for k in range(2):
        for core in range(2):
            arrived(window.at[k, pl.ds(TAPS // 2 + EP * core, EP), :], halo_recv.at[k, core])
        start(
            remote(
                window.at[k, pl.ds(TAPS // 2, TAPS // 2), :],
                window.at[k, pl.ds(0, TAPS // 2), :],
                far_send.at[k],
                far_recv.at[k],
                dev(next_chip, h),
            )
        )
        if k == 0:
            build(1)

    def slot(k, at):
        return gathered[k].at[at]

    def filter_and_send(k):
        arrived(window.at[k, pl.ds(pl.multiple_of(TAPS + EP * other, EP), EP), :], own_recv.at[k])
        near = jnp.dot(
            toeplitz[k, :, TAPS // 2 :], window[k, TAPS // 2 :, :], preferred_element_type=F32
        )
        arrived(window.at[k, pl.ds(0, TAPS // 2), :], far_recv.at[k])
        far = jnp.dot(
            toeplitz[k, :, : TAPS // 2], window[k, : TAPS // 2, :], preferred_element_type=F32
        )
        gathered[k][x] = (near + far).T.astype(BF16)
        start(remote(slot(k, x), slot(k, x), col_send.at[k, 0], col_recv.at[k, 0], dev(chip, h, x_up)))
        start(remote(slot(k, x), slot(k, x), col_send.at[k, 1], col_recv.at[k, 1], dev(chip, h, x_down)))

    def relay(k):
        if k == 0:
            arrived(slot(k, x_down), col_recv.at[k, 0])
            start(remote(slot(k, x_down), slot(k, x_down), col_send.at[k, 2], col_recv.at[k, 2], dev(chip, h, x_up)))
            arrived(slot(k, x_up), col_recv.at[k, 1])
        else:
            arrived(slot(k, x_up), col_recv.at[k, 1])
            start(remote(slot(k, x_up), slot(k, x_up), col_send.at[k, 2], col_recv.at[k, 2], dev(chip, h, x_down)))
            arrived(slot(k, x_down), col_recv.at[k, 0])

    def block_of(wanted):
        found = jnp.int32(0)
        for d in range(1, BLOCKS):
            found = jnp.where(ids_ref[d] == wanted, d, found)
        return found

    def scale(k):
        arrived(slot(k, lax.rem(x + 2, NX)), col_recv.at[k, 2])
        row_weight = jnp.concatenate([weights_all[0, k : k + 1], weights_all[1, k : k + 1]], axis=1)
        mine = gathered[k][block_of(x)].astype(F32) * row_weight
        scaled[k, h] = mine.astype(BF16)
        start(remote(scaled.at[k, h], scaled.at[k, h], q_send.at[k], q_recv.at[k], dev(chip, other)))

    def multiply(k):
        arrived(scaled.at[k, other], q_recv.at[k])
        right = scaled[k].reshape(CB, 2 * EP)
        for b in range(BLOCKS):
            left = gathered[k][block_of(b)]
            product = lax.dot_general(
                left, right, (((1,), (1,)), ((), ())), preferred_element_type=F32
            ).reshape(NZ, 8, CB)
            if k == 0:
                gram[:, b] = product
            else:
                gram[:, b] += product

    filter_and_send(0)
    relay(0)
    filter_and_send(1)
    scale(0)
    relay(1)
    multiply(0)
    scale(1)
    multiply(1)

    size = BLOCKS // PARTS
    for step in range(1, NZ // 2 + 1):
        for part in range(PARTS):
            piece = pl.ds(part * size, size)
            for way in range(2):
                slots, send_sem, recv_sem = (
                    (up_slots, up_send, up_recv) if way == 0 else (down_slots, down_send, down_recv)
                )
                if way == 1 and step == NZ // 2:
                    continue
                if way == 0:
                    dest = lax.rem(z + NZ // 2 + 1 - step, NZ)
                else:
                    dest = lax.rem(z + NZ // 2 + step, NZ)
                if step == 1:
                    src = gram.at[dest, piece]
                else:
                    src = slots.at[step - 2, piece]
                    arrived(src, recv_sem.at[step - 2, part])
                    slots[step - 2, piece] += gram[dest, piece]
                start(
                    remote(
                        src,
                        slots.at[step - 1, piece],
                        send_sem.at[step - 1, part],
                        recv_sem.at[step - 1, part],
                        dev(z_up if way == 0 else z_down, h),
                    )
                )
    for part in range(PARTS):
        piece = pl.ds(part * size, size)
        arrived(up_slots.at[NZ // 2 - 1, piece], up_recv.at[NZ // 2 - 1, part])
        arrived(down_slots.at[NZ // 2 - 2, piece], down_recv.at[NZ // 2 - 2, part])
        total[piece] = gram[z, piece] + up_slots[NZ // 2 - 1, piece] + down_slots[NZ // 2 - 2, piece]

    for b in range(BLOCKS):
        for core in range(2):
            remote_one = jnp.logical_not(
                jnp.logical_and(jnp.logical_and(2 * b + h == y, on_diagonal), h == core)
            )
            copy = remote(
                total.at[b],
                y_slots.at[y],
                y_send.at[b, core],
                y_recv.at[y],
                dev((2 * b + h) * NZ + z, core),
            )

            @pl.when(remote_one)
            def _():
                copy.start()

    @pl.when(on_diagonal)
    def _():
        y_slots[y] = total[y // 2]

    for source in range(NY):

        @pl.when(jnp.logical_not(jnp.logical_and(source == y, on_diagonal)))
        def _():
            arrived(y_slots.at[source], y_recv.at[source])

    result = y_slots[0]
    for source in range(1, NY):
        result = result + y_slots[source]
    out_ref[...] = jnp.where(h == 0, result[:4], result[4:]) * (1.0 / 65536.0)

    for copy in sends:
        copy.wait_send()
    for b in range(BLOCKS):
        for core in range(2):
            remote_one = jnp.logical_not(
                jnp.logical_and(jnp.logical_and(2 * b + h == y, on_diagonal), h == core)
            )

            @pl.when(remote_one)
            def _():
                remote(
                    total.at[b],
                    y_slots.at[y],
                    y_send.at[b, core],
                    y_recv.at[y],
                    dev((2 * b + h) * NZ + z, core),
                ).wait_send()


def body(design, filter_taps, segment, valid_flags, weights, block_ids):
    seg_count = filter_taps.shape[0]
    selector = (segment[:, None] == jnp.arange(seg_count, dtype=jnp.int32)[None, :]).astype(BF16)
    tap_rows = jnp.einsum("ts,skj->ktj", selector, filter_taps, preferred_element_type=F32).astype(BF16)
    rows = jnp.transpose(design, (1, 0, 2))
    row_weight = weights * valid_flags[None, :].astype(F32)
    vmem = pl.BlockSpec(memory_space=pltpu.VMEM)
    dma = pltpu.SemaphoreType.DMA
    steps = NZ // 2
    return pl.pallas_call(
        kernel,
        out_shape=jax.ShapeDtypeStruct((4, CB), F32),
        in_specs=[vmem, vmem, vmem, pl.BlockSpec(memory_space=pltpu.SMEM)],
        out_specs=vmem,
        scratch_shapes=[
            pltpu.VMEM((2, TAPS + 2 * EP, HALF), BF16),
            pltpu.VMEM((2, 2, EP, TAPS), BF16),
            pltpu.VMEM((2, 2, EP), F32),
            pltpu.VMEM((2, 2 * EP, TAPS + 2 * EP), BF16),
            pltpu.VMEM((NX, HALF, 2 * EP), BF16),
            pltpu.VMEM((NX, HALF, 2 * EP), BF16),
            pltpu.VMEM((2, 2, HALF, 2 * EP), BF16),
            pltpu.VMEM((NZ, BLOCKS, 8, CB), F32),
            pltpu.VMEM((steps, BLOCKS, 8, CB), F32),
            pltpu.VMEM((steps - 1, BLOCKS, 8, CB), F32),
            pltpu.VMEM((NY, 8, CB), F32),
            pltpu.VMEM((BLOCKS, 8, CB), F32),
            dma((2,)),
            dma((2,)),
            dma((2, 2)),
            dma((2, 2)),
            dma((2,)),
            dma((2,)),
            dma((2,)),
            dma((2,)),
            dma((2, 3)),
            dma((2, 3)),
            dma((2,)),
            dma((2,)),
            dma((steps, PARTS)),
            dma((steps, PARTS)),
            dma((steps - 1, PARTS)),
            dma((steps - 1, PARTS)),
            dma((BLOCKS, 2)),
            dma((NY,)),
        ],
        compiler_params=pltpu.CompilerParams(collective_id=0, has_side_effects=True),
    )(rows, tap_rows, row_weight, block_ids)


def solution(mesh):
    return jax.shard_map(
        body,
        mesh=mesh,
        in_specs=(P("tm", None, "col"), P(), P("tm"), P("tm"), P(None, "tm"), P()),
        out_specs=P("tm", "col"),
        check_vma=False,
    )
```

```python
import jax
import jax.numpy as jnp
from jax import lax
from jax.experimental import pallas as pl
from jax.experimental.pallas import tpu as pltpu
from jax.sharding import PartitionSpec as P

MESH = pl.DeviceIdType.MESH
NY, NZ, NX = 8, 16, 4
CHIPS = NY * NZ
EP = 128
CB = 256
HALF = 128
TAPS = 512
SEGS = 256
BLOCKS = 4
SPAN = 2 * EP
WINDOW = TAPS + SPAN
F32 = jnp.float32
BF16 = jnp.bfloat16

COLLECTOR = {8: 5, 7: 5, -7: -5, 6: 5, -6: -5, 4: 5, -4: -5, 3: 5, -3: -5, 2: 0, -2: 0, 1: 0, -1: 0}
SOURCES = list(COLLECTOR)


def kernel(
    design_ref,
    taps_ref,
    segment_ref,
    valid_ref,
    weight_ref,
    ids_ref,
    out_ref,
    rows,
    window,
    side_weight,
    side_segment,
    toeplitz,
    gathered_0,
    gathered_1,
    scaled,
    gram_z,
    gram_y,
    z_slots,
    middle,
    z_tops,
    total_z,
    z_final,
    y_slots,
    total_y,
    y_final,
    near_send,
    near_recv,
    far_send,
    far_recv,
    own_send,
    own_recv,
    side_send,
    side_recv,
    col_send,
    col_recv,
    q_send,
    q_recv,
    z_send,
    z_recv,
    top_send,
    top_recv,
    zf_send,
    zf_recv,
    y_send,
    y_recv,
    yf_send,
    yf_recv,
    token,
):
    tm = lax.axis_index("tm")
    x = lax.axis_index("col")
    h = lax.rem(tm, 2)
    chip = tm // 2
    z = lax.rem(chip, NZ)
    y = chip // NZ
    other = 1 - h
    y_core = lax.rem(y, 2)
    keeps = h == y_core
    gathered = (gathered_0, gathered_1)

    def dev(chip_at, core, x_at=x):
        return {"tm": chip_at * 2 + core, "col": x_at}

    def along_z(offset, core=h):
        return dev(y * NZ + lax.rem(z + offset + NZ, NZ), core)

    def along_y(offset, core=h):
        return dev(lax.rem(y + offset + NY, NY) * NZ + z, core)

    def remote(src, dst, send_sem, recv_sem, device):
        return pltpu.make_async_remote_copy(
            src_ref=src, dst_ref=dst, send_sem=send_sem, recv_sem=recv_sem, device_id=device, device_id_type=MESH
        )

    pair = dev(chip, other)
    next_chip = lax.rem(chip + 1, CHIPS)
    prev_chip = lax.rem(chip + CHIPS - 1, CHIPS)
    x_up, x_down = lax.rem(x + 1, NX), lax.rem(x + NX - 1, NX)
    x_far = lax.rem(x + 2, NX)

    sends = []

    def start(copy):
        copy.start()
        sends.append(copy)

    def arrived(dst, recv_sem):
        remote(dst, dst, own_send.at[0], recv_sem, pair).wait_recv()

    def tell(which, devices):
        for device in devices:
            pl.semaphore_signal(token.at[which], inc=1, device_id=device, device_id_type=MESH)

    barrier = pltpu.get_barrier_semaphore()
    greeted = [
        pair,
        dev(prev_chip, 0),
        dev(prev_chip, 1),
        dev(chip, h, x_up),
        dev(chip, h, x_down),
        along_z(1),
        along_z(-1),
        along_y(1),
        along_y(-1),
    ]
    for device in greeted:
        pl.semaphore_signal(barrier, inc=1, device_id=device, device_id_type=MESH)
    for k in range(2):
        rows[k] = design_ref[:, k, :]
    pl.semaphore_wait(barrier, len(greeted))

    own_rows = pl.ds(pl.multiple_of(TAPS + EP * h, EP), EP)
    near_rows = pl.ds(pl.multiple_of(TAPS // 2 + EP * h, EP), EP)
    my_cols = pl.ds(pl.multiple_of(HALF * h, HALF), HALF)
    other_cols = pl.ds(pl.multiple_of(HALF * other, HALF), HALF)

    for k in range(2):
        for core in range(2):
            start(
                remote(
                    rows.at[k, :, pl.ds(HALF * core, HALF)],
                    window.at[k, near_rows, :],
                    near_send.at[k, core],
                    near_recv.at[k, h],
                    dev(next_chip, core),
                )
            )
    side_weight[h] = weight_ref[...] * valid_ref[...].astype(F32)
    start(remote(segment_ref, side_segment.at[h], side_send.at[0], side_recv.at[0], pair))
    for k in range(2):
        start(
            remote(
                rows.at[k, :, other_cols], window.at[k, own_rows, :], own_send.at[k], own_recv.at[k], pair
            )
        )
    tell(0, [along_z(1), along_z(-1)])
    tell(1, [along_y(1), along_y(-1)])
    for k in range(2):
        window[k, own_rows, :] = rows[k, :, my_cols]
    side_segment[h] = segment_ref[...]
    start(remote(side_weight.at[h], side_weight.at[h], side_send.at[1], side_recv.at[1], pair))

    flip = (
        lax.broadcasted_iota(jnp.int32, (TAPS, TAPS), 0) + lax.broadcasted_iota(jnp.int32, (TAPS, TAPS), 1)
        == TAPS - 1
    ).astype(F32).astype(BF16)
    first_row = jnp.where(chip == 0, TAPS, jnp.where(chip == 1, TAPS // 2, 0))
    lane = lax.broadcasted_iota(jnp.int32, (SPAN, WINDOW), 1)
    arrived(side_segment.at[other], side_recv.at[0])
    segments = jnp.concatenate([side_segment[0], side_segment[1]], axis=1)
    selector = (lax.broadcasted_iota(jnp.int32, (SEGS, SPAN), 0) == segments).astype(F32).astype(BF16)

    def build(k):
        tap_rows = lax.dot_general(
            selector, taps_ref[:, k, :], (((0,), (0,)), ((), ())), preferred_element_type=F32
        ).astype(BF16)
        flipped = jnp.dot(tap_rows, flip, preferred_element_type=F32)
        wide = jnp.concatenate([flipped, jnp.zeros((SPAN, SPAN), F32)], axis=1)
        skewed = pltpu.roll(wide, 1, 1, stride=1, stride_axis=0)
        toeplitz[k] = jnp.where(lane >= first_row, skewed, 0.0).astype(BF16)

    def pass_on(k):
        for core in range(2):
            arrived(window.at[k, pl.ds(TAPS // 2 + EP * core, EP), :], near_recv.at[k, core])
        start(
            remote(
                window.at[k, pl.ds(TAPS // 2, TAPS // 2), :],
                window.at[k, pl.ds(0, TAPS // 2), :],
                far_send.at[k],
                far_recv.at[k],
                dev(next_chip, h),
            )
        )

    build(0)
    pass_on(0)
    pl.semaphore_wait(token.at[0], 2)
    pl.semaphore_wait(token.at[1], 2)
    tell(2, [along_z(2), along_z(-2)])
    tell(3, [along_y(2), along_y(-2)])
    pass_on(1)
    build(1)
    pl.semaphore_wait(token.at[2], 2)
    pl.semaphore_wait(token.at[3], 2)
    tell(4, [along_z(4), along_z(-4)])

    def piece(k, at, part):
        return gathered[k].at[at, pl.ds(part * HALF // 2, HALF // 2)]

    def send_piece(k, at, part, which, x_to):
        start(remote(piece(k, at, part), piece(k, at, part), col_send.at[k, which], col_recv.at[k, which], dev(chip, h, x_to)))

    def filter_and_send(k):
        arrived(window.at[k, pl.ds(pl.multiple_of(TAPS + EP * other, EP), EP), :], own_recv.at[k])
        near = jnp.dot(toeplitz[k, :, TAPS // 2 :], window[k, TAPS // 2 :, :], preferred_element_type=F32)
        arrived(window.at[k, pl.ds(0, TAPS // 2), :], far_recv.at[k])
        far = jnp.dot(toeplitz[k, :, : TAPS // 2], window[k, : TAPS // 2, :], preferred_element_type=F32)
        gathered[k][x] = (near + far).T.astype(BF16)
        send_piece(k, x, 0, 0, x_up)
        send_piece(k, x, 1, 1, x_down)
        send_piece(k, x, 1, 2, x_up)
        send_piece(k, x, 0, 3, x_down)

    def relay(k):
        arrived(piece(k, x_down, 0), col_recv.at[k, 0])
        send_piece(k, x_down, 0, 4, x_up)
        arrived(piece(k, x_up, 1), col_recv.at[k, 1])
        send_piece(k, x_up, 1, 5, x_down)

    def block_of(wanted):
        found = jnp.int32(0)
        for d in range(1, BLOCKS):
            found = jnp.where(ids_ref[d] == wanted, d, found)
        return found

    def scale(k):
        arrived(piece(k, x_down, 1), col_recv.at[k, 2])
        arrived(piece(k, x_up, 0), col_recv.at[k, 3])
        arrived(piece(k, x_far, 0), col_recv.at[k, 4])
        arrived(piece(k, x_far, 1), col_recv.at[k, 5])
        row_weight = jnp.concatenate([side_weight[0, k : k + 1], side_weight[1, k : k + 1]], axis=1)
        scaled[k, h] = (gathered[k][block_of(x)].astype(F32) * row_weight).astype(BF16)
        start(remote(scaled.at[k, h], scaled.at[k, h], q_send.at[k], q_recv.at[k], pair))

    def y_copy(b):
        step = lax.rem(2 * b + h - y + NY, NY)
        return remote(gram_y.at[b], y_slots.at[step], y_send.at[b], y_recv.at[step], dev((2 * b + h) * NZ + z, h))

    def multiply(k):
        arrived(scaled.at[k, other], q_recv.at[k])
        right = scaled[k].reshape(CB, SPAN)
        for b in range(BLOCKS):
            product = lax.dot_general(
                gathered[k][block_of(b)], right, (((1,), (1,)), ((), ())), preferred_element_type=F32
            ).reshape(NZ, 8, CB)
            if k == 0:
                gram_z[:, b] = product[:, :, :HALF]
                gram_y[b] = product[:, :, HALF:]
            else:
                gram_z[:, b] += product[:, :, :HALF]
                gram_y[b] += product[:, :, HALF:]

    filter_and_send(0)
    pl.semaphore_wait(token.at[4], 2)
    tell(5, [pair])
    relay(0)
    filter_and_send(1)
    arrived(side_weight.at[other], side_recv.at[1])
    scale(0)
    relay(1)
    multiply(0)
    scale(1)
    pl.semaphore_wait(token.at[5], 1)
    multiply(1)

    for index, s in enumerate(SOURCES):
        if index == 4:
            for b in range(BLOCKS):

                @pl.when(2 * b + h != y)
                def _():
                    y_copy(b).start()

        start(
            remote(
                gram_z.at[lax.rem(z - s + NZ, NZ)],
                z_slots.at[index],
                z_send.at[index],
                z_recv.at[index],
                along_z(COLLECTOR[s] - s),
            )
        )

    def collect(into, own):
        added = gram_z[own]
        for index, s in enumerate(SOURCES):
            if COLLECTOR[s] == into:
                arrived(z_slots.at[index], z_recv.at[index])
                added = added + z_slots[index]
        return added

    for index, place in enumerate((-5, 5)):
        middle[index] = collect(place, lax.rem(z - place + NZ, NZ))
        start(
            remote(middle.at[index], z_tops.at[index], top_send.at[index], top_recv.at[index], along_z(-place))
        )

    def yf_copies():
        out = [remote(total_y.at[z], y_final.at[0], yf_send.at[0, 0], yf_recv.at[0], pair)]
        for step in range(1, NZ):
            for core in range(2):
                out.append(
                    remote(
                        total_y.at[lax.rem(z + step, NZ)],
                        y_final.at[step],
                        yf_send.at[step, core],
                        yf_recv.at[step],
                        along_z(step, core),
                    )
                )
        return out

    @pl.when(keeps)
    def _():
        added = gram_y[y // 2]
        for step in range(1, NY):
            arrived(y_slots.at[step], y_recv.at[step])
            added = added + y_slots[step]
        total_y[...] = added
        copies = yf_copies()
        for step in (8, 7, 9, 6, 10, 5, 11, 4, 12, 3, 13, 2, 14, 1, 15):
            copies[2 * step - 1].start()
            copies[2 * step].start()
        copies[0].start()
        y_final[0] = total_y[z]

    summed = collect(0, z)
    for index in range(2):
        arrived(z_tops.at[index], top_recv.at[index])
        summed = summed + z_tops[index]
    total_z[...] = summed

    def zf_copy(b, core):
        step = lax.rem(2 * b + h - y + NY, NY)
        return remote(
            total_z.at[b], z_final.at[step], zf_send.at[b, core], zf_recv.at[step], dev((2 * b + h) * NZ + z, core)
        )

    def for_each_zf(act):
        for b in range(BLOCKS):
            for core in range(2):

                @pl.when(jnp.logical_not(jnp.logical_and(2 * b + h == y, h == core)))
                def _():
                    act(zf_copy(b, core))

    for_each_zf(lambda copy: copy.start())

    @pl.when(keeps)
    def _():
        z_final[0] = total_z[y // 2]

    @pl.when(jnp.logical_not(keeps))
    def _():
        arrived(y_final.at[0], yf_recv.at[0])
        arrived(z_final.at[0], zf_recv.at[0])

    right = y_final[0]
    for step in range(1, NZ):
        arrived(y_final.at[step], yf_recv.at[step])
        right = right + y_final[step]
    left = z_final[0]
    for step in range(1, NY):
        arrived(z_final.at[step], zf_recv.at[step])
        left = left + z_final[step]
    result = jnp.concatenate([left, right], axis=1) * (1.0 / 65536.0)
    out_ref[...] = jnp.where(h == 0, result[:4], result[4:])

    for copy in sends:
        copy.wait_send()
    for b in range(BLOCKS):

        @pl.when(2 * b + h != y)
        def _():
            y_copy(b).wait_send()

    for_each_zf(lambda copy: copy.wait_send())

    @pl.when(keeps)
    def _():
        for copy in yf_copies():
            copy.wait_send()


def body(design, filter_taps, segment, valid_flags, weights, block_ids):
    vmem = pl.BlockSpec(memory_space=pltpu.VMEM)
    dma = pltpu.SemaphoreType.DMA
    kinds = len(SOURCES)
    return pl.pallas_call(
        kernel,
        out_shape=jax.ShapeDtypeStruct((4, CB), F32),
        in_specs=[vmem] * 5 + [pl.BlockSpec(memory_space=pltpu.SMEM)],
        out_specs=vmem,
        scratch_shapes=[
            pltpu.VMEM((2, EP, CB), BF16),
            pltpu.VMEM((2, WINDOW, HALF), BF16),
            pltpu.VMEM((2, 2, EP), F32),
            pltpu.VMEM((2, 1, EP), jnp.int32),
            pltpu.VMEM((2, SPAN, WINDOW), BF16),
            pltpu.VMEM((NX, HALF, SPAN), BF16),
            pltpu.VMEM((NX, HALF, SPAN), BF16),
            pltpu.VMEM((2, 2, HALF, SPAN), BF16),
            pltpu.VMEM((NZ, BLOCKS, 8, HALF), F32),
            pltpu.VMEM((BLOCKS, NZ, 8, HALF), F32),
            pltpu.VMEM((kinds, BLOCKS, 8, HALF), F32),
            pltpu.VMEM((2, BLOCKS, 8, HALF), F32),
            pltpu.VMEM((2, BLOCKS, 8, HALF), F32),
            pltpu.VMEM((BLOCKS, 8, HALF), F32),
            pltpu.VMEM((NY, 8, HALF), F32),
            pltpu.VMEM((NY, NZ, 8, HALF), F32),
            pltpu.VMEM((NZ, 8, HALF), F32),
            pltpu.VMEM((NZ, 8, HALF), F32),
            dma((2, 2)),
            dma((2, 2)),
            dma((2,)),
            dma((2,)),
            dma((2,)),
            dma((2,)),
            dma((2,)),
            dma((2,)),
            dma((2, 6)),
            dma((2, 6)),
            dma((2,)),
            dma((2,)),
            dma((kinds,)),
            dma((kinds,)),
            dma((2,)),
            dma((2,)),
            dma((BLOCKS, 2)),
            dma((NY,)),
            dma((BLOCKS,)),
            dma((NY,)),
            dma((NZ, 2)),
            dma((NZ,)),
            pltpu.SemaphoreType.REGULAR((6,)),
        ],
        compiler_params=pltpu.CompilerParams(collective_id=0, has_side_effects=True),
    )(design, filter_taps, segment.reshape(1, EP), valid_flags.reshape(1, EP), weights, block_ids)


def solution(mesh):
    return jax.shard_map(
        body,
        mesh=mesh,
        in_specs=(P("tm", None, "col"), P(), P("tm"), P("tm"), P(None, "tm"), P()),
        out_specs=P("tm", "col"),
        check_vma=False,
    )
```

```python
import jax
import jax.numpy as jnp
from jax import lax
from jax.experimental import pallas as pl
from jax.experimental.pallas import tpu as pltpu
from jax.sharding import PartitionSpec as P

MESH = pl.DeviceIdType.MESH
NY, NZ, NX = 8, 16, 4
CHIPS = NY * NZ
EP = 128
CB = 256
HALF = 128
TAPS = 512
SEGS = 256
BLOCKS = 4
SPAN = 2 * EP
WINDOW = TAPS + SPAN
F32 = jnp.float32
BF16 = jnp.bfloat16

COLLECTOR = {8: 5, 7: 5, -7: -5, 6: 5, -6: -5, 4: 5, -4: -5, 3: 5, -3: -5, 2: 0, -2: 0, 1: 0, -1: 0}
SOURCES = list(COLLECTOR)


def kernel(
    design_in,
    taps_in,
    segment_in,
    valid_in,
    weight_in,
    ids_in,
    out_ref,
    design_ref,
    taps_ref,
    segment_ref,
    valid_ref,
    weight_ref,
    ids_ref,
    rows,
    window,
    side_mine,
    side_weight,
    side_segment,
    toeplitz,
    gathered_0,
    gathered_1,
    scaled,
    gram_z,
    gram_y,
    z_slots,
    middle,
    z_tops,
    total_z,
    z_final,
    y_slots,
    total_y,
    y_final,
    first_send,
    first_recv,
    last_send,
    last_recv,
    own_send,
    own_recv,
    side_send,
    side_recv,
    col_send,
    col_recv,
    q_send,
    q_recv,
    z_send,
    z_recv,
    top_send,
    top_recv,
    zf_send,
    zf_recv,
    y_send,
    y_recv,
    yf_send,
    yf_recv,
    token,
    load_sem,
):
    loads = [
        pltpu.make_async_copy(src, dst, load_sem.at[index])
        for index, (src, dst) in enumerate(
            (
                (design_in, design_ref),
                (segment_in, segment_ref),
                (valid_in, valid_ref),
                (weight_in, weight_ref),
                (taps_in, taps_ref),
                (ids_in, ids_ref),
            )
        )
    ]
    for load in loads:
        load.start()

    tm = lax.axis_index("tm")
    x = lax.axis_index("col")
    h = lax.rem(tm, 2)
    chip = tm // 2
    z = lax.rem(chip, NZ)
    y = chip // NZ
    other = 1 - h
    y_core = lax.rem(y, 2)
    keeps = h == y_core
    gathered = (gathered_0, gathered_1)

    def dev(chip_at, core, x_at=x):
        return {"tm": chip_at * 2 + core, "col": x_at}

    def along_z(offset, core=h):
        return dev(y * NZ + lax.rem(z + offset + NZ, NZ), core)

    def along_y(offset, core=h):
        return dev(lax.rem(y + offset + NY, NY) * NZ + z, core)

    def remote(src, dst, send_sem, recv_sem, device):
        return pltpu.make_async_remote_copy(
            src_ref=src, dst_ref=dst, send_sem=send_sem, recv_sem=recv_sem, device_id=device, device_id_type=MESH
        )

    pair = dev(chip, other)
    next_chip = lax.rem(chip + 1, CHIPS)
    prev_chip = lax.rem(chip + CHIPS - 1, CHIPS)
    x_up, x_down = lax.rem(x + 1, NX), lax.rem(x + NX - 1, NX)
    x_far = lax.rem(x + 2, NX)

    sends = []

    def start(copy):
        copy.start()
        sends.append(copy)

    def arrived(dst, recv_sem):
        remote(dst, dst, own_send.at[0], recv_sem, pair).wait_recv()

    def tell(which, devices):
        for device in devices:
            pl.semaphore_signal(token.at[which], inc=1, device_id=device, device_id_type=MESH)

    barrier = pltpu.get_barrier_semaphore()
    greeted = [
        pair,
        dev(prev_chip, 0),
        dev(prev_chip, 1),
        dev(next_chip, 0),
        dev(next_chip, 1),
        dev(chip, h, x_up),
        dev(chip, h, x_down),
        along_z(1),
        along_z(-1),
        along_y(1),
        along_y(-1),
    ]
    for device in greeted:
        pl.semaphore_signal(barrier, inc=1, device_id=device, device_id_type=MESH)
    loads[0].wait()
    for k in range(2):
        rows[k] = design_ref[:, k, :]
    pl.semaphore_wait(barrier, len(greeted))

    first_rows = pl.ds(pl.multiple_of(EP * h, EP), EP)
    own_rows = pl.ds(pl.multiple_of(SPAN + EP * h, EP), EP)
    last_rows = pl.ds(pl.multiple_of(2 * SPAN + EP * h, EP), EP)
    my_cols = pl.ds(pl.multiple_of(HALF * h, HALF), HALF)
    other_cols = pl.ds(pl.multiple_of(HALF * other, HALF), HALF)

    for load in loads[1:4]:
        load.wait()
    side_mine[...] = weight_ref[...] * valid_ref[...].astype(F32)
    for core in range(2):
        start(
            remote(
                segment_ref, side_segment.at[h], side_send.at[0, core], side_recv.at[0, h], dev(prev_chip, core)
            )
        )
    for k in range(2):
        for core in range(2):
            half = rows.at[k, :, pl.ds(HALF * core, HALF)]
            start(
                remote(
                    half, window.at[k, last_rows, :], last_send.at[k, core], last_recv.at[k, h], dev(prev_chip, core)
                )
            )
            start(
                remote(
                    half, window.at[k, first_rows, :], first_send.at[k, core], first_recv.at[k, h], dev(next_chip, core)
                )
            )
        start(
            remote(
                rows.at[k, :, other_cols], window.at[k, own_rows, :], own_send.at[k], own_recv.at[k], pair
            )
        )
    for core in range(2):
        start(
            remote(side_mine, side_weight.at[h], side_send.at[1, core], side_recv.at[1, h], dev(prev_chip, core))
        )
    tell(0, [along_z(1), along_z(-1)])
    tell(1, [along_y(1), along_y(-1)])
    for k in range(2):
        window[k, own_rows, :] = rows[k, :, my_cols]

    flip = (
        lax.broadcasted_iota(jnp.int32, (TAPS, TAPS), 0) + lax.broadcasted_iota(jnp.int32, (TAPS, TAPS), 1)
        == TAPS - 1
    ).astype(F32).astype(BF16)
    first_row = jnp.where(chip == CHIPS - 1, TAPS, jnp.where(chip == 0, SPAN, 0))
    lane = lax.broadcasted_iota(jnp.int32, (SPAN, WINDOW), 1)
    for core in range(2):
        arrived(side_segment.at[core], side_recv.at[0, core])
    segments = jnp.concatenate([side_segment[0], side_segment[1]], axis=1)
    selector = (lax.broadcasted_iota(jnp.int32, (SEGS, SPAN), 0) == segments).astype(F32).astype(BF16)

    def build(k):
        tap_rows = lax.dot_general(
            selector, taps_ref[:, k, :], (((0,), (0,)), ((), ())), preferred_element_type=F32
        ).astype(BF16)
        flipped = jnp.dot(tap_rows, flip, preferred_element_type=F32)
        wide = jnp.concatenate([flipped, jnp.zeros((SPAN, SPAN), F32)], axis=1)
        skewed = pltpu.roll(wide, 1, 1, stride=1, stride_axis=0)
        toeplitz[k] = jnp.where(lane >= first_row, skewed, 0.0).astype(BF16)

    loads[4].wait()
    loads[5].wait()
    build(0)
    pl.semaphore_wait(token.at[0], 2)
    pl.semaphore_wait(token.at[1], 2)
    tell(2, [along_z(2), along_z(-2)])
    tell(3, [along_y(2), along_y(-2)])

    def piece(k, at, side):
        return gathered[k].at[at, pl.ds(side * HALF // 2, HALF // 2)]

    def send_piece(k, at, side, which, x_to):
        start(remote(piece(k, at, side), piece(k, at, side), col_send.at[k, which], col_recv.at[k, which], dev(chip, h, x_to)))

    def part(k, at):
        span = pl.ds(SPAN * at, SPAN)
        return jnp.dot(toeplitz[k, :, span], window[k, span, :], preferred_element_type=F32)

    def filter_and_send(k):
        arrived(window.at[k, pl.ds(pl.multiple_of(SPAN + EP * other, EP), EP), :], own_recv.at[k])
        added = part(k, 1)
        for core in range(2):
            arrived(window.at[k, pl.ds(EP * core, EP), :], first_recv.at[k, core])
        added = added + part(k, 0)
        for core in range(2):
            arrived(window.at[k, pl.ds(2 * SPAN + EP * core, EP), :], last_recv.at[k, core])
        added = added + part(k, 2)
        gathered[k][x] = added.T.astype(BF16)
        send_piece(k, x, 0, 0, x_up)
        send_piece(k, x, 1, 1, x_down)
        send_piece(k, x, 1, 2, x_up)
        send_piece(k, x, 0, 3, x_down)

    def relay(k):
        arrived(piece(k, x_down, 0), col_recv.at[k, 0])
        send_piece(k, x_down, 0, 4, x_up)
        arrived(piece(k, x_up, 1), col_recv.at[k, 1])
        send_piece(k, x_up, 1, 5, x_down)

    def block_of(wanted):
        found = jnp.int32(0)
        for d in range(1, BLOCKS):
            found = jnp.where(ids_ref[d] == wanted, d, found)
        return found

    def scale(k):
        arrived(piece(k, x_down, 1), col_recv.at[k, 2])
        arrived(piece(k, x_up, 0), col_recv.at[k, 3])
        arrived(piece(k, x_far, 0), col_recv.at[k, 4])
        arrived(piece(k, x_far, 1), col_recv.at[k, 5])
        row_weight = jnp.concatenate([side_weight[0, k : k + 1], side_weight[1, k : k + 1]], axis=1)
        scaled[k, h] = (gathered[k][block_of(x)].astype(F32) * row_weight).astype(BF16)
        start(remote(scaled.at[k, h], scaled.at[k, h], q_send.at[k], q_recv.at[k], pair))

    def y_copy(b):
        step = lax.rem(2 * b + h - y + NY, NY)
        return remote(gram_y.at[b], y_slots.at[step], y_send.at[b], y_recv.at[step], dev((2 * b + h) * NZ + z, h))

    def multiply(k):
        arrived(scaled.at[k, other], q_recv.at[k])
        right = scaled[k].reshape(CB, SPAN)
        for b in range(BLOCKS):
            product = lax.dot_general(
                gathered[k][block_of(b)], right, (((1,), (1,)), ((), ())), preferred_element_type=F32
            ).reshape(NZ, 8, CB)
            if k == 0:
                gram_z[:, b] = product[:, :, :HALF]
                gram_y[b] = product[:, :, HALF:]
            else:
                gram_z[:, b] += product[:, :, :HALF]
                gram_y[b] += product[:, :, HALF:]

    filter_and_send(0)
    build(1)
    pl.semaphore_wait(token.at[2], 2)
    pl.semaphore_wait(token.at[3], 2)
    tell(4, [along_z(4), along_z(-4)])
    filter_and_send(1)
    relay(0)
    pl.semaphore_wait(token.at[4], 2)
    tell(5, [pair])
    for core in range(2):
        arrived(side_weight.at[core], side_recv.at[1, core])
    scale(0)
    relay(1)
    multiply(0)
    scale(1)
    pl.semaphore_wait(token.at[5], 1)
    multiply(1)

    for index, s in enumerate(SOURCES):
        if index == 4:
            for b in range(BLOCKS):

                @pl.when(2 * b + h != y)
                def _():
                    y_copy(b).start()

        start(
            remote(
                gram_z.at[lax.rem(z - s + NZ, NZ)],
                z_slots.at[index],
                z_send.at[index],
                z_recv.at[index],
                along_z(COLLECTOR[s] - s),
            )
        )

    def collect(into, own):
        added = gram_z[own]
        for index, s in enumerate(SOURCES):
            if COLLECTOR[s] == into:
                arrived(z_slots.at[index], z_recv.at[index])
                added = added + z_slots[index]
        return added

    for index, place in enumerate((-5, 5)):
        middle[index] = collect(place, lax.rem(z - place + NZ, NZ))
        start(
            remote(middle.at[index], z_tops.at[index], top_send.at[index], top_recv.at[index], along_z(-place))
        )

    def yf_copies():
        out = [remote(total_y.at[z, other], y_final.at[0], yf_send.at[0, 0], yf_recv.at[0], pair)]
        for step in range(1, NZ):
            for core in range(2):
                out.append(
                    remote(
                        total_y.at[lax.rem(z + step, NZ), core],
                        y_final.at[step],
                        yf_send.at[step, core],
                        yf_recv.at[step],
                        along_z(step, core),
                    )
                )
        return out

    @pl.when(keeps)
    def _():
        added = gram_y[y // 2]
        for step in range(1, NY):
            arrived(y_slots.at[step], y_recv.at[step])
            added = added + y_slots[step]
        total_y[:, 0] = added[:, :4]
        total_y[:, 1] = added[:, 4:]
        copies = yf_copies()
        for step in (8, 7, 9, 6, 10, 5, 11, 4, 12, 3, 13, 2, 14, 1, 15):
            copies[2 * step - 1].start()
            copies[2 * step].start()
        copies[0].start()
        y_final[0] = total_y[z, h]

    summed = collect(0, z)
    for index in range(2):
        arrived(z_tops.at[index], top_recv.at[index])
        summed = summed + z_tops[index]
    total_z[:, 0] = summed[:, :4]
    total_z[:, 1] = summed[:, 4:]

    def zf_copy(b, core):
        step = lax.rem(2 * b + h - y + NY, NY)
        return remote(
            total_z.at[b, core], z_final.at[step], zf_send.at[b, core], zf_recv.at[step], dev((2 * b + h) * NZ + z, core)
        )

    def for_each_zf(act):
        for b in range(BLOCKS):
            for core in range(2):

                @pl.when(jnp.logical_not(jnp.logical_and(2 * b + h == y, h == core)))
                def _():
                    act(zf_copy(b, core))

    for_each_zf(lambda copy: copy.start())

    @pl.when(keeps)
    def _():
        z_final[0] = total_z[y // 2, h]

    @pl.when(jnp.logical_not(keeps))
    def _():
        arrived(y_final.at[0], yf_recv.at[0])
        arrived(z_final.at[0], zf_recv.at[0])

    right = y_final[0]
    for step in range(1, NZ):
        arrived(y_final.at[step], yf_recv.at[step])
        right = right + y_final[step]
    left = z_final[0]
    for step in range(1, NY):
        arrived(z_final.at[step], zf_recv.at[step])
        left = left + z_final[step]
    out_ref[...] = jnp.concatenate([left, right], axis=1) * (1.0 / 65536.0)

    for copy in sends:
        copy.wait_send()
    for b in range(BLOCKS):

        @pl.when(2 * b + h != y)
        def _():
            y_copy(b).wait_send()

    for_each_zf(lambda copy: copy.wait_send())

    @pl.when(keeps)
    def _():
        for copy in yf_copies():
            copy.wait_send()


def body(design, filter_taps, segment, valid_flags, weights, block_ids):
    vmem = pl.BlockSpec(memory_space=pltpu.VMEM)
    dma = pltpu.SemaphoreType.DMA
    kinds = len(SOURCES)
    return pl.pallas_call(
        kernel,
        out_shape=jax.ShapeDtypeStruct((4, CB), F32),
        in_specs=[pl.BlockSpec(memory_space=pl.ANY)] * 6,
        out_specs=vmem,
        scratch_shapes=[
            pltpu.VMEM((EP, 2, CB), BF16),
            pltpu.VMEM((SEGS, 2, TAPS), BF16),
            pltpu.VMEM((1, EP), jnp.int32),
            pltpu.VMEM((1, EP), jnp.int32),
            pltpu.VMEM((2, EP), F32),
            pltpu.SMEM((BLOCKS,), jnp.int32),
            pltpu.VMEM((2, EP, CB), BF16),
            pltpu.VMEM((2, WINDOW, HALF), BF16),
            pltpu.VMEM((2, EP), F32),
            pltpu.VMEM((2, 2, EP), F32),
            pltpu.VMEM((2, 1, EP), jnp.int32),
            pltpu.VMEM((2, SPAN, WINDOW), BF16),
            pltpu.VMEM((NX, HALF, SPAN), BF16),
            pltpu.VMEM((NX, HALF, SPAN), BF16),
            pltpu.VMEM((2, 2, HALF, SPAN), BF16),
            pltpu.VMEM((NZ, BLOCKS, 8, HALF), F32),
            pltpu.VMEM((BLOCKS, NZ, 8, HALF), F32),
            pltpu.VMEM((kinds, BLOCKS, 8, HALF), F32),
            pltpu.VMEM((2, BLOCKS, 8, HALF), F32),
            pltpu.VMEM((2, BLOCKS, 8, HALF), F32),
            pltpu.VMEM((BLOCKS, 2, 4, HALF), F32),
            pltpu.VMEM((NY, 4, HALF), F32),
            pltpu.VMEM((NY, NZ, 8, HALF), F32),
            pltpu.VMEM((NZ, 2, 4, HALF), F32),
            pltpu.VMEM((NZ, 4, HALF), F32),
            dma((2, 2)),
            dma((2, 2)),
            dma((2, 2)),
            dma((2, 2)),
            dma((2,)),
            dma((2,)),
            dma((2, 2)),
            dma((2, 2)),
            dma((2, 6)),
            dma((2, 6)),
            dma((2,)),
            dma((2,)),
            dma((kinds,)),
            dma((kinds,)),
            dma((2,)),
            dma((2,)),
            dma((BLOCKS, 2)),
            dma((NY,)),
            dma((BLOCKS,)),
            dma((NY,)),
            dma((NZ, 2)),
            dma((NZ,)),
            pltpu.SemaphoreType.REGULAR((6,)),
            dma((6,)),
        ],
        compiler_params=pltpu.CompilerParams(collective_id=0, has_side_effects=True),
    )(design, filter_taps, segment.reshape(1, EP), valid_flags.reshape(1, EP), weights, block_ids)


def solution(mesh):
    return jax.shard_map(
        body,
        mesh=mesh,
        in_specs=(P("tm", None, "col"), P(), P("tm"), P("tm"), P(None, "tm"), P()),
        out_specs=P("tm", "col"),
        check_vma=False,
    )
```

```python
import jax
import jax.numpy as jnp
from jax import lax
from jax.experimental import pallas as pl
from jax.experimental.pallas import tpu as pltpu
from jax.sharding import PartitionSpec as P

MESH = pl.DeviceIdType.MESH
NY, NZ, NX = 8, 16, 4
CHIPS = NY * NZ
EP = 128
CB = 256
HALF = 128
TAPS = 512
SEGS = 256
BLOCKS = 4
SPAN = 2 * EP
WINDOW = TAPS + SPAN
F32 = jnp.float32
BF16 = jnp.bfloat16

COLLECTOR = {8: 5, 7: 5, -7: -5, 6: 5, -6: -5, 4: 5, -4: -5, 3: 5, -3: -5, 2: 0, -2: 0, 1: 0, -1: 0}
SOURCES = list(COLLECTOR)


def kernel(
    design_in,
    taps_in,
    segment_in,
    valid_in,
    weight_in,
    ids_in,
    out_ref,
    design_ref,
    taps_ref,
    segment_ref,
    valid_ref,
    weight_ref,
    ids_ref,
    rows,
    window,
    side_mine,
    side_weight,
    side_segment,
    toeplitz,
    gathered_0,
    gathered_1,
    scaled,
    gram_z,
    gram_y,
    z_slots,
    middle,
    z_tops,
    total_z,
    z_final,
    y_slots,
    total_y,
    y_final,
    first_send,
    first_recv,
    last_send,
    last_recv,
    own_send,
    own_recv,
    side_send,
    side_recv,
    col_send,
    col_recv,
    q_send,
    q_recv,
    z_send,
    z_recv,
    top_send,
    top_recv,
    zf_send,
    zf_recv,
    y_send,
    y_recv,
    yf_send,
    yf_recv,
    token,
    load_sem,
):
    loads = [
        pltpu.make_async_copy(src, dst, load_sem.at[index])
        for index, (src, dst) in enumerate(
            (
                (design_in, design_ref),
                (segment_in, segment_ref),
                (valid_in, valid_ref),
                (weight_in, weight_ref),
                (taps_in, taps_ref),
                (ids_in, ids_ref),
            )
        )
    ]
    for load in loads:
        load.start()

    tm = lax.axis_index("tm")
    x = lax.axis_index("col")
    h = lax.rem(tm, 2)
    chip = tm // 2
    z = lax.rem(chip, NZ)
    y = chip // NZ
    other = 1 - h
    y_core = lax.rem(y, 2)
    keeps = h == y_core
    gathered = (gathered_0, gathered_1)

    def dev(chip_at, core, x_at=x):
        return {"tm": chip_at * 2 + core, "col": x_at}

    def along_z(offset, core=h):
        return dev(y * NZ + lax.rem(z + offset + NZ, NZ), core)

    def along_y(offset, core=h):
        return dev(lax.rem(y + offset + NY, NY) * NZ + z, core)

    def remote(src, dst, send_sem, recv_sem, device):
        return pltpu.make_async_remote_copy(
            src_ref=src, dst_ref=dst, send_sem=send_sem, recv_sem=recv_sem, device_id=device, device_id_type=MESH
        )

    pair = dev(chip, other)
    next_chip = lax.rem(chip + 1, CHIPS)
    prev_chip = lax.rem(chip + CHIPS - 1, CHIPS)
    x_up, x_down = lax.rem(x + 1, NX), lax.rem(x + NX - 1, NX)
    x_far = lax.rem(x + 2, NX)

    sends = []

    def start(copy):
        copy.start()
        sends.append(copy)

    def arrived(dst, recv_sem):
        remote(dst, dst, own_send.at[0], recv_sem, pair).wait_recv()

    def tell(which, devices):
        for device in devices:
            pl.semaphore_signal(token.at[which], inc=1, device_id=device, device_id_type=MESH)

    barrier = pltpu.get_barrier_semaphore()
    greeted = [
        pair,
        dev(prev_chip, 0),
        dev(prev_chip, 1),
        dev(next_chip, 0),
        dev(next_chip, 1),
        dev(chip, h, x_up),
        dev(chip, h, x_down),
        along_z(1),
        along_z(-1),
        along_y(1),
        along_y(-1),
    ]
    for device in greeted:
        pl.semaphore_signal(barrier, inc=1, device_id=device, device_id_type=MESH)
    loads[0].wait()
    for k in range(2):
        rows[k] = design_ref[:, k, :]
    pl.semaphore_wait(barrier, len(greeted))

    first_rows = pl.ds(pl.multiple_of(EP * h, EP), EP)
    own_rows = pl.ds(pl.multiple_of(SPAN + EP * h, EP), EP)
    last_rows = pl.ds(pl.multiple_of(2 * SPAN + EP * h, EP), EP)
    my_cols = pl.ds(pl.multiple_of(HALF * h, HALF), HALF)
    other_cols = pl.ds(pl.multiple_of(HALF * other, HALF), HALF)

    for load in loads[1:4]:
        load.wait()
    side_mine[...] = weight_ref[...] * valid_ref[...].astype(F32)
    for core in range(2):
        start(
            remote(
                segment_ref, side_segment.at[h], side_send.at[0, core], side_recv.at[0, h], dev(prev_chip, core)
            )
        )
    for k in range(2):
        for core in range(2):
            half = rows.at[k, :, pl.ds(HALF * core, HALF)]
            start(
                remote(
                    half, window.at[k, last_rows, :], last_send.at[k, core], last_recv.at[k, h], dev(prev_chip, core)
                )
            )
            start(
                remote(
                    half, window.at[k, first_rows, :], first_send.at[k, core], first_recv.at[k, h], dev(next_chip, core)
                )
            )
        start(
            remote(
                rows.at[k, :, other_cols], window.at[k, own_rows, :], own_send.at[k], own_recv.at[k], pair
            )
        )
    for core in range(2):
        start(
            remote(side_mine, side_weight.at[h], side_send.at[1, core], side_recv.at[1, h], dev(prev_chip, core))
        )
    tell(0, [along_z(1), along_z(-1)])
    tell(1, [along_y(1), along_y(-1)])
    for k in range(2):
        window[k, own_rows, :] = rows[k, :, my_cols]

    flip = (
        lax.broadcasted_iota(jnp.int32, (TAPS, TAPS), 0) + lax.broadcasted_iota(jnp.int32, (TAPS, TAPS), 1)
        == TAPS - 1
    ).astype(F32).astype(BF16)
    first_row = jnp.where(chip == CHIPS - 1, TAPS, jnp.where(chip == 0, SPAN, 0))
    lane = lax.broadcasted_iota(jnp.int32, (SPAN, WINDOW), 1)
    for core in range(2):
        arrived(side_segment.at[core], side_recv.at[0, core])
    segments = jnp.concatenate([side_segment[0], side_segment[1]], axis=1)
    selector = (lax.broadcasted_iota(jnp.int32, (SEGS, SPAN), 0) == segments).astype(F32).astype(BF16)

    def build(k):
        tap_rows = lax.dot_general(
            selector, taps_ref[:, k, :], (((0,), (0,)), ((), ())), preferred_element_type=F32
        ).astype(BF16)
        flipped = jnp.dot(tap_rows, flip, preferred_element_type=F32)
        wide = jnp.concatenate([flipped, jnp.zeros((SPAN, SPAN), F32)], axis=1)
        skewed = pltpu.roll(wide, 1, 1, stride=1, stride_axis=0)
        toeplitz[k] = jnp.where(lane >= first_row, skewed, 0.0).astype(BF16)

    loads[4].wait()
    loads[5].wait()
    build(0)
    pl.semaphore_wait(token.at[0], 2)
    pl.semaphore_wait(token.at[1], 2)
    tell(2, [along_z(2), along_z(-2)])
    tell(3, [along_y(2), along_y(-2)])

    def piece(k, at, side):
        return gathered[k].at[at, pl.ds(side * HALF // 2, HALF // 2)]

    def send_piece(k, at, side, which, x_to):
        start(remote(piece(k, at, side), piece(k, at, side), col_send.at[k, which], col_recv.at[k, which], dev(chip, h, x_to)))

    def part(k, at):
        span = pl.ds(SPAN * at, SPAN)
        return jnp.dot(toeplitz[k, :, span], window[k, span, :], preferred_element_type=F32)

    def filter_and_send(k):
        arrived(window.at[k, pl.ds(pl.multiple_of(SPAN + EP * other, EP), EP), :], own_recv.at[k])
        added = part(k, 1)
        for core in range(2):
            arrived(window.at[k, pl.ds(EP * core, EP), :], first_recv.at[k, core])
        added = added + part(k, 0)
        for core in range(2):
            arrived(window.at[k, pl.ds(2 * SPAN + EP * core, EP), :], last_recv.at[k, core])
        added = added + part(k, 2)
        gathered[k][x] = added.T.astype(BF16)
        send_piece(k, x, 0, 0, x_up)
        send_piece(k, x, 1, 1, x_down)
        send_piece(k, x, 1, 2, x_up)
        send_piece(k, x, 0, 3, x_down)

    def relay(k):
        arrived(piece(k, x_down, 0), col_recv.at[k, 0])
        send_piece(k, x_down, 0, 4, x_up)
        arrived(piece(k, x_up, 1), col_recv.at[k, 1])
        send_piece(k, x_up, 1, 5, x_down)

    def block_of(wanted):
        found = jnp.int32(0)
        for d in range(1, BLOCKS):
            found = jnp.where(ids_ref[d] == wanted, d, found)
        return found

    def scale(k):
        arrived(piece(k, x_down, 1), col_recv.at[k, 2])
        arrived(piece(k, x_up, 0), col_recv.at[k, 3])
        arrived(piece(k, x_far, 0), col_recv.at[k, 4])
        arrived(piece(k, x_far, 1), col_recv.at[k, 5])
        row_weight = jnp.concatenate([side_weight[0, k : k + 1], side_weight[1, k : k + 1]], axis=1)
        scaled[k, h] = (gathered[k][block_of(x)].astype(F32) * row_weight).astype(BF16)
        start(remote(scaled.at[k, h], scaled.at[k, h], q_send.at[k], q_recv.at[k], pair))

    first_step = jnp.where(keeps, NY // 2, NY // 2 - 1)

    def place(b):
        return lax.rem(2 * b + h - y - first_step + 2 * NY, NY) // 2

    def y_copy(at, part):
        step = lax.rem(2 * at + first_step, NY)
        span = pl.ds(part * NZ // 2, NZ // 2)
        return remote(
            gram_y.at[at, span],
            y_slots.at[step, span],
            y_send.at[at, part],
            y_recv.at[step, part],
            along_y(2 * at + first_step),
        )

    def for_each_y(part, act):
        for at in range(BLOCKS):
            if at == 2:

                @pl.when(jnp.logical_not(keeps))
                def _():
                    act(y_copy(at, part))

            else:
                act(y_copy(at, part))

    def multiply(k):
        arrived(scaled.at[k, other], q_recv.at[k])
        right = scaled[k].reshape(CB, SPAN)
        for b in range(BLOCKS):
            product = lax.dot_general(
                gathered[k][block_of(b)], right, (((1,), (1,)), ((), ())), preferred_element_type=F32
            ).reshape(NZ, 8, CB)
            at = place(b)
            if k == 0:
                gram_z[:, at] = product[:, :, :HALF]
            else:
                gram_z[:, at] += product[:, :, :HALF]
            for row in range(NZ):
                turned = lax.rem(row - z - 4 + 2 * NZ, NZ)
                if k == 0:
                    gram_y[at, turned] = product[row, :, HALF:]
                else:
                    gram_y[at, turned] += product[row, :, HALF:]

    filter_and_send(0)
    build(1)
    pl.semaphore_wait(token.at[2], 2)
    pl.semaphore_wait(token.at[3], 2)
    tell(4, [along_z(4), along_z(-4)])
    filter_and_send(1)
    relay(0)
    pl.semaphore_wait(token.at[4], 2)
    tell(5, [pair])
    for core in range(2):
        arrived(side_weight.at[core], side_recv.at[1, core])
    relay(1)
    scale(0)
    scale(1)
    multiply(0)
    pl.semaphore_wait(token.at[5], 1)
    multiply(1)

    def z_pair(part):
        return pl.ds(2 * part, 2)

    def send_z(part, near):
        for index, s in enumerate(SOURCES):
            if (COLLECTOR[s] == 0) == near:
                start(
                    remote(
                        gram_z.at[lax.rem(z - s + NZ, NZ), z_pair(part)],
                        z_slots.at[index, z_pair(part)],
                        z_send.at[index, part],
                        z_recv.at[index, part],
                        along_z(COLLECTOR[s] - s),
                    )
                )

    send_z(0, False)
    for_each_y(0, lambda copy: copy.start())
    send_z(1, False)
    for_each_y(1, lambda copy: copy.start())
    send_z(0, True)
    send_z(1, True)

    def collect(into, own, part):
        added = gram_z[own, z_pair(part)]
        for index, s in enumerate(SOURCES):
            if COLLECTOR[s] == into:
                arrived(z_slots.at[index, z_pair(part)], z_recv.at[index, part])
                added = added + z_slots[index, z_pair(part)]
        return added

    for part in range(2):
        for index, to in enumerate((-5, 5)):
            middle[index, z_pair(part)] = collect(to, lax.rem(z - to + NZ, NZ), part)
            start(
                remote(
                    middle.at[index, z_pair(part)],
                    z_tops.at[index, z_pair(part)],
                    top_send.at[index, part],
                    top_recv.at[index, part],
                    along_z(-to),
                )
            )

    def yf_copies(part):
        out = []
        for step in ((8, 7, 9, 6, 10, 5, 11, 4), (12, 3, 13, 2, 14, 1, 15, 0))[part]:
            for core in range(2):
                if step:
                    out.append(
                        remote(
                            total_y.at[(step - 4) % NZ, core],
                            y_final.at[step],
                            yf_send.at[step, core],
                            yf_recv.at[step],
                            along_z(step, core),
                        )
                    )
        if part == 1:
            out.append(remote(total_y.at[NZ - 4, other], y_final.at[0], yf_send.at[0, 0], yf_recv.at[0], pair))
        return out

    @pl.when(keeps)
    def _():
        for part in range(2):
            span = pl.ds(part * NZ // 2, NZ // 2)
            added = gram_y[2, span]
            for step in range(1, NY):
                arrived(y_slots.at[step, span], y_recv.at[step, part])
                added = added + y_slots[step, span]
            total_y[span, 0] = added[:, :4]
            total_y[span, 1] = added[:, 4:]
            for copy in yf_copies(part):
                copy.start()
        y_final[0] = total_y[NZ - 4, h]

    def zf_copy(at, core):
        step = lax.rem(2 * at + first_step, NY)
        return remote(
            total_z.at[at, core],
            z_final.at[step],
            zf_send.at[at, core],
            zf_recv.at[step],
            along_y(2 * at + first_step, core),
        )

    def for_each_zf(part, act):
        for at in (2 * part, 2 * part + 1):
            for core in range(2):
                if at == 2:

                    @pl.when(jnp.logical_not(jnp.logical_and(keeps, h == core)))
                    def _():
                        act(zf_copy(at, core))

                else:
                    act(zf_copy(at, core))

    for part in range(2):
        summed = collect(0, z, part)
        for index in range(2):
            arrived(z_tops.at[index, z_pair(part)], top_recv.at[index, part])
            summed = summed + z_tops[index, z_pair(part)]
        total_z[z_pair(part), 0] = summed[:, :4]
        total_z[z_pair(part), 1] = summed[:, 4:]
        for_each_zf(part, lambda copy: copy.start())

    @pl.when(keeps)
    def _():
        z_final[0] = total_z[2, h]

    @pl.when(jnp.logical_not(keeps))
    def _():
        arrived(y_final.at[0], yf_recv.at[0])
        arrived(z_final.at[0], zf_recv.at[0])

    right = y_final[0]
    for step in range(1, NZ):
        arrived(y_final.at[step], yf_recv.at[step])
        right = right + y_final[step]
    left = z_final[0]
    for step in range(1, NY):
        arrived(z_final.at[step], zf_recv.at[step])
        left = left + z_final[step]
    out_ref[...] = jnp.concatenate([left, right], axis=1) * (1.0 / 65536.0)

    for copy in sends:
        copy.wait_send()
    for part in range(2):
        for_each_y(part, lambda copy: copy.wait_send())
        for_each_zf(part, lambda copy: copy.wait_send())

    @pl.when(keeps)
    def _():
        for part in range(2):
            for copy in yf_copies(part):
                copy.wait_send()


def body(design, filter_taps, segment, valid_flags, weights, block_ids):
    vmem = pl.BlockSpec(memory_space=pltpu.VMEM)
    dma = pltpu.SemaphoreType.DMA
    kinds = len(SOURCES)
    return pl.pallas_call(
        kernel,
        out_shape=jax.ShapeDtypeStruct((4, CB), F32),
        in_specs=[pl.BlockSpec(memory_space=pl.ANY)] * 6,
        out_specs=vmem,
        scratch_shapes=[
            pltpu.VMEM((EP, 2, CB), BF16),
            pltpu.VMEM((SEGS, 2, TAPS), BF16),
            pltpu.VMEM((1, EP), jnp.int32),
            pltpu.VMEM((1, EP), jnp.int32),
            pltpu.VMEM((2, EP), F32),
            pltpu.SMEM((BLOCKS,), jnp.int32),
            pltpu.VMEM((2, EP, CB), BF16),
            pltpu.VMEM((2, WINDOW, HALF), BF16),
            pltpu.VMEM((2, EP), F32),
            pltpu.VMEM((2, 2, EP), F32),
            pltpu.VMEM((2, 1, EP), jnp.int32),
            pltpu.VMEM((2, SPAN, WINDOW), BF16),
            pltpu.VMEM((NX, HALF, SPAN), BF16),
            pltpu.VMEM((NX, HALF, SPAN), BF16),
            pltpu.VMEM((2, 2, HALF, SPAN), BF16),
            pltpu.VMEM((NZ, BLOCKS, 8, HALF), F32),
            pltpu.VMEM((BLOCKS, NZ, 8, HALF), F32),
            pltpu.VMEM((kinds, BLOCKS, 8, HALF), F32),
            pltpu.VMEM((2, BLOCKS, 8, HALF), F32),
            pltpu.VMEM((2, BLOCKS, 8, HALF), F32),
            pltpu.VMEM((BLOCKS, 2, 4, HALF), F32),
            pltpu.VMEM((NY, 4, HALF), F32),
            pltpu.VMEM((NY, NZ, 8, HALF), F32),
            pltpu.VMEM((NZ, 2, 4, HALF), F32),
            pltpu.VMEM((NZ, 4, HALF), F32),
            dma((2, 2)),
            dma((2, 2)),
            dma((2, 2)),
            dma((2, 2)),
            dma((2,)),
            dma((2,)),
            dma((2, 2)),
            dma((2, 2)),
            dma((2, 6)),
            dma((2, 6)),
            dma((2,)),
            dma((2,)),
            dma((kinds, 2)),
            dma((kinds, 2)),
            dma((2, 2)),
            dma((2, 2)),
            dma((BLOCKS, 2)),
            dma((NY,)),
            dma((BLOCKS, 2)),
            dma((NY, 2)),
            dma((NZ, 2)),
            dma((NZ,)),
            pltpu.SemaphoreType.REGULAR((6,)),
            dma((6,)),
        ],
        compiler_params=pltpu.CompilerParams(collective_id=0, has_side_effects=True),
    )(design, filter_taps, segment.reshape(1, EP), valid_flags.reshape(1, EP), weights, block_ids)


def solution(mesh):
    return jax.shard_map(
        body,
        mesh=mesh,
        in_specs=(P("tm", None, "col"), P(), P("tm"), P("tm"), P(None, "tm"), P()),
        out_specs=P("tm", "col"),
        check_vma=False,
    )
```

```python
import jax
import jax.numpy as jnp
from jax import lax
from jax.experimental import pallas as pl
from jax.experimental.pallas import tpu as pltpu
from jax.sharding import PartitionSpec as P

MESH = pl.DeviceIdType.MESH
NY, NZ, NX = 8, 16, 4
CHIPS = NY * NZ
EP = 128
CB = 256
HALF = 128
TAPS = 512
SEGS = 256
BLOCKS = 4
SPAN = 2 * EP
WINDOW = TAPS + SPAN
GRANT = 54 * 1024 * 1024 - 96 * 1024
F32 = jnp.float32
BF16 = jnp.bfloat16

COLLECTOR = {8: 5, 7: 5, -7: -5, 6: 5, -6: -5, 4: 5, -4: -5, 3: 5, -3: -5, 2: 0, -2: 0, 1: 0, -1: 0}
SOURCES = list(COLLECTOR)


def kernel(
    design_in,
    taps_in,
    segment_in,
    valid_in,
    weight_in,
    ids_in,
    out_ref,
    design_ref,
    taps_ref,
    segment_ref,
    valid_ref,
    weight_ref,
    ids_ref,
    rows,
    window,
    side_mine,
    side_weight,
    side_segment,
    toeplitz,
    gathered_0,
    gathered_1,
    scaled,
    gram_z,
    gram_y,
    z_slots,
    middle,
    z_tops,
    total_z,
    z_final,
    y_slots,
    total_y,
    y_final,
    first_send,
    first_recv,
    last_send,
    last_recv,
    own_send,
    own_recv,
    side_send,
    side_recv,
    col_send,
    col_recv,
    q_send,
    q_recv,
    z_send,
    z_recv,
    top_send,
    top_recv,
    zf_send,
    zf_recv,
    y_send,
    y_recv,
    yf_send,
    yf_recv,
    token,
    load_sem,
):
    loads = [
        pltpu.make_async_copy(src, dst, load_sem.at[index])
        for index, (src, dst) in enumerate(
            (
                (design_in, design_ref),
                (segment_in, segment_ref),
                (valid_in, valid_ref),
                (weight_in, weight_ref),
                (taps_in, taps_ref),
                (ids_in, ids_ref),
            )
        )
    ]
    for load in loads:
        load.start()

    tm = lax.axis_index("tm")
    x = lax.axis_index("col")
    h = lax.rem(tm, 2)
    chip = tm // 2
    z = lax.rem(chip, NZ)
    y = chip // NZ
    other = 1 - h
    y_core = lax.rem(y, 2)
    keeps = h == y_core
    gathered = (gathered_0, gathered_1)

    def dev(chip_at, core, x_at=x):
        return {"tm": chip_at * 2 + core, "col": x_at}

    def along_z(offset, core=h):
        return dev(y * NZ + lax.rem(z + offset + NZ, NZ), core)

    def along_y(offset, core=h):
        return dev(lax.rem(y + offset + NY, NY) * NZ + z, core)

    def remote(src, dst, send_sem, recv_sem, device):
        return pltpu.make_async_remote_copy(
            src_ref=src, dst_ref=dst, send_sem=send_sem, recv_sem=recv_sem, device_id=device, device_id_type=MESH
        )

    pair = dev(chip, other)
    next_chip = lax.rem(chip + 1, CHIPS)
    prev_chip = lax.rem(chip + CHIPS - 1, CHIPS)
    x_up, x_down = lax.rem(x + 1, NX), lax.rem(x + NX - 1, NX)
    x_far = lax.rem(x + 2, NX)

    sends = []

    def start(copy):
        copy.start()
        sends.append(copy)

    def arrived(dst, recv_sem):
        remote(dst, dst, own_send.at[0], recv_sem, pair).wait_recv()

    def tell(which, devices):
        for device in devices:
            pl.semaphore_signal(token.at[which], inc=1, device_id=device, device_id_type=MESH)

    barrier = pltpu.get_barrier_semaphore()
    greeted = [
        pair,
        dev(prev_chip, 0),
        dev(prev_chip, 1),
        dev(next_chip, 0),
        dev(next_chip, 1),
        dev(chip, h, x_up),
        dev(chip, h, x_down),
        along_z(1),
        along_z(-1),
        along_y(1),
        along_y(-1),
    ]
    for device in greeted:
        pl.semaphore_signal(barrier, inc=1, device_id=device, device_id_type=MESH)
    loads[0].wait()
    rows[0] = design_ref[:, 0, :]
    pl.semaphore_wait(barrier, len(greeted))

    first_rows = pl.ds(pl.multiple_of(EP * h, EP), EP)
    own_rows = pl.ds(pl.multiple_of(SPAN + EP * h, EP), EP)
    last_rows = pl.ds(pl.multiple_of(2 * SPAN + EP * h, EP), EP)
    my_cols = pl.ds(pl.multiple_of(HALF * h, HALF), HALF)
    other_cols = pl.ds(pl.multiple_of(HALF * other, HALF), HALF)

    for k in range(2):
        if k == 1:
            for load in loads[1:4]:
                load.wait()
            side_mine[...] = weight_ref[...] * valid_ref[...].astype(F32)
            for core in range(2):
                start(
                    remote(
                        segment_ref, side_segment.at[h], side_send.at[0, core], side_recv.at[0, h], dev(prev_chip, core)
                    )
                )
            rows[1] = design_ref[:, 1, :]
        for core in range(2):
            half = rows.at[k, :, pl.ds(HALF * core, HALF)]
            start(
                remote(
                    half, window.at[k, last_rows, :], last_send.at[k, core], last_recv.at[k, h], dev(prev_chip, core)
                )
            )
            start(
                remote(
                    half, window.at[k, first_rows, :], first_send.at[k, core], first_recv.at[k, h], dev(next_chip, core)
                )
            )
        start(
            remote(
                rows.at[k, :, other_cols], window.at[k, own_rows, :], own_send.at[k], own_recv.at[k], pair
            )
        )
    for core in range(2):
        start(
            remote(side_mine, side_weight.at[h], side_send.at[1, core], side_recv.at[1, h], dev(prev_chip, core))
        )
    tell(0, [along_z(1), along_z(-1)])
    tell(1, [along_y(1), along_y(-1)])
    for k in range(2):
        window[k, own_rows, :] = rows[k, :, my_cols]

    flip = (
        lax.broadcasted_iota(jnp.int32, (TAPS, TAPS), 0) + lax.broadcasted_iota(jnp.int32, (TAPS, TAPS), 1)
        == TAPS - 1
    ).astype(F32).astype(BF16)
    first_row = jnp.where(chip == CHIPS - 1, TAPS, jnp.where(chip == 0, SPAN, 0))
    lane = lax.broadcasted_iota(jnp.int32, (SPAN, WINDOW), 1)
    for core in range(2):
        arrived(side_segment.at[core], side_recv.at[0, core])
    segments = jnp.concatenate([side_segment[0], side_segment[1]], axis=1)
    selector = (lax.broadcasted_iota(jnp.int32, (SEGS, SPAN), 0) == segments).astype(F32).astype(BF16)

    def build(k):
        tap_rows = lax.dot_general(
            selector, taps_ref[:, k, :], (((0,), (0,)), ((), ())), preferred_element_type=F32
        ).astype(BF16)
        flipped = jnp.dot(tap_rows, flip, preferred_element_type=F32)
        wide = jnp.concatenate([flipped, jnp.zeros((SPAN, SPAN), F32)], axis=1)
        skewed = pltpu.roll(wide, 1, 1, stride=1, stride_axis=0)
        toeplitz[k] = jnp.where(lane >= first_row, skewed, 0.0).astype(BF16)

    loads[4].wait()
    loads[5].wait()
    build(0)
    pl.semaphore_wait(token.at[0], 2)
    pl.semaphore_wait(token.at[1], 2)
    tell(2, [along_z(2), along_z(-2)])
    tell(3, [along_y(2), along_y(-2)])

    def piece(k, at, side):
        return gathered[k].at[at, pl.ds(side * HALF // 2, HALF // 2)]

    def send_piece(k, at, side, which, x_to):
        start(remote(piece(k, at, side), piece(k, at, side), col_send.at[k, which], col_recv.at[k, which], dev(chip, h, x_to)))

    def part(k, at):
        span = pl.ds(SPAN * at, SPAN)
        return jnp.dot(toeplitz[k, :, span], window[k, span, :], preferred_element_type=F32)

    def filter_and_send(k):
        arrived(window.at[k, pl.ds(pl.multiple_of(SPAN + EP * other, EP), EP), :], own_recv.at[k])
        added = part(k, 1)
        for core in range(2):
            arrived(window.at[k, pl.ds(EP * core, EP), :], first_recv.at[k, core])
        added = added + part(k, 0)
        for core in range(2):
            arrived(window.at[k, pl.ds(2 * SPAN + EP * core, EP), :], last_recv.at[k, core])
        added = added + part(k, 2)
        gathered[k][x] = added.T.astype(BF16)
        send_piece(k, x, 0, 0, x_up)
        send_piece(k, x, 1, 1, x_down)
        send_piece(k, x, 1, 2, x_up)
        send_piece(k, x, 0, 3, x_down)

    def relay(k):
        arrived(piece(k, x_down, 0), col_recv.at[k, 0])
        send_piece(k, x_down, 0, 4, x_up)
        arrived(piece(k, x_up, 1), col_recv.at[k, 1])
        send_piece(k, x_up, 1, 5, x_down)

    def block_of(wanted):
        found = jnp.int32(0)
        for d in range(1, BLOCKS):
            found = jnp.where(ids_ref[d] == wanted, d, found)
        return found

    def scale(k):
        arrived(piece(k, x_down, 1), col_recv.at[k, 2])
        arrived(piece(k, x_up, 0), col_recv.at[k, 3])
        arrived(piece(k, x_far, 0), col_recv.at[k, 4])
        arrived(piece(k, x_far, 1), col_recv.at[k, 5])
        row_weight = jnp.concatenate([side_weight[0, k : k + 1], side_weight[1, k : k + 1]], axis=1)
        scaled[k, h] = (gathered[k][block_of(x)].astype(F32) * row_weight).astype(BF16)
        start(remote(scaled.at[k, h], scaled.at[k, h], q_send.at[k], q_recv.at[k], pair))

    first_step = jnp.where(keeps, NY // 2, NY // 2 - 1)

    def place(b):
        return lax.rem(2 * b + h - y - first_step + 2 * NY, NY) // 2

    def y_copy(at, part):
        step = lax.rem(2 * at + first_step, NY)
        span = pl.ds(part * NZ // 2, NZ // 2)
        return remote(
            gram_y.at[at, span],
            y_slots.at[step, span],
            y_send.at[at, part],
            y_recv.at[step, part],
            along_y(2 * at + first_step),
        )

    def for_each_y(part, act):
        for at in range(BLOCKS):
            if at == 2:

                @pl.when(jnp.logical_not(keeps))
                def _():
                    act(y_copy(at, part))

            else:
                act(y_copy(at, part))

    def multiply(k):
        arrived(scaled.at[k, other], q_recv.at[k])
        right = scaled[k].reshape(CB, SPAN)
        for b in range(BLOCKS):
            product = lax.dot_general(
                gathered[k][block_of(b)], right, (((1,), (1,)), ((), ())), preferred_element_type=F32
            ).reshape(NZ, 8, CB)
            at = place(b)
            if k == 0:
                gram_z[:, at] = product[:, :, :HALF]
            else:
                gram_z[:, at] += product[:, :, :HALF]
            for row in range(NZ):
                turned = lax.rem(row - z - 4 + 2 * NZ, NZ)
                if k == 0:
                    gram_y[at, turned] = product[row, :, HALF:]
                else:
                    gram_y[at, turned] += product[row, :, HALF:]

    filter_and_send(0)
    build(1)
    pl.semaphore_wait(token.at[2], 2)
    pl.semaphore_wait(token.at[3], 2)
    tell(4, [along_z(4), along_z(-4)])
    filter_and_send(1)
    relay(0)
    pl.semaphore_wait(token.at[4], 2)
    tell(5, [pair])
    for core in range(2):
        arrived(side_weight.at[core], side_recv.at[1, core])
    relay(1)
    scale(0)
    scale(1)
    multiply(0)
    pl.semaphore_wait(token.at[5], 1)
    multiply(1)

    def z_pair(part):
        return pl.ds(2 * part, 2)

    def send_z(part, near):
        for index, s in enumerate(SOURCES):
            if (COLLECTOR[s] == 0) == near:
                start(
                    remote(
                        gram_z.at[lax.rem(z - s + NZ, NZ), z_pair(part)],
                        z_slots.at[index, z_pair(part)],
                        z_send.at[index, part],
                        z_recv.at[index, part],
                        along_z(COLLECTOR[s] - s),
                    )
                )

    send_z(0, False)
    for_each_y(0, lambda copy: copy.start())
    send_z(1, False)
    for_each_y(1, lambda copy: copy.start())
    send_z(0, True)
    send_z(1, True)

    def collect(into, own, part):
        added = gram_z[own, z_pair(part)]
        for index, s in enumerate(SOURCES):
            if COLLECTOR[s] == into:
                arrived(z_slots.at[index, z_pair(part)], z_recv.at[index, part])
                added = added + z_slots[index, z_pair(part)]
        return added

    for part in range(2):
        for index, to in enumerate((-5, 5)):
            middle[index, z_pair(part)] = collect(to, lax.rem(z - to + NZ, NZ), part)
            start(
                remote(
                    middle.at[index, z_pair(part)],
                    z_tops.at[index, z_pair(part)],
                    top_send.at[index, part],
                    top_recv.at[index, part],
                    along_z(-to),
                )
            )

    def yf_copies(part):
        out = []
        for step in ((8, 7, 9, 6, 10, 5, 11, 4), (12, 3, 13, 2, 14, 1, 15, 0))[part]:
            for core in range(2):
                if step:
                    out.append(
                        remote(
                            total_y.at[(step - 4) % NZ, core],
                            y_final.at[step],
                            yf_send.at[step, core],
                            yf_recv.at[step],
                            along_z(step, core),
                        )
                    )
        if part == 1:
            out.append(remote(total_y.at[NZ - 4, other], y_final.at[0], yf_send.at[0, 0], yf_recv.at[0], pair))
        return out

    @pl.when(keeps)
    def _():
        for part in range(2):
            span = pl.ds(part * NZ // 2, NZ // 2)
            added = gram_y[2, span]
            for step in range(1, NY):
                arrived(y_slots.at[step, span], y_recv.at[step, part])
                added = added + y_slots[step, span]
            total_y[span, 0] = added[:, :4]
            total_y[span, 1] = added[:, 4:]
            for copy in yf_copies(part):
                copy.start()
        y_final[0] = total_y[NZ - 4, h]

    def zf_copy(at, core):
        step = lax.rem(2 * at + first_step, NY)
        return remote(
            total_z.at[at, core],
            z_final.at[step],
            zf_send.at[at, core],
            zf_recv.at[step],
            along_y(2 * at + first_step, core),
        )

    def for_each_zf(part, act):
        for at in (2 * part, 2 * part + 1):
            for core in range(2):
                if at == 2:

                    @pl.when(jnp.logical_not(jnp.logical_and(keeps, h == core)))
                    def _():
                        act(zf_copy(at, core))

                else:
                    act(zf_copy(at, core))

    for part in range(2):
        summed = collect(0, z, part)
        for index in range(2):
            arrived(z_tops.at[index, z_pair(part)], top_recv.at[index, part])
            summed = summed + z_tops[index, z_pair(part)]
        total_z[z_pair(part), 0] = summed[:, :4]
        total_z[z_pair(part), 1] = summed[:, 4:]
        for_each_zf(part, lambda copy: copy.start())

    @pl.when(keeps)
    def _():
        z_final[0] = total_z[2, h]

    @pl.when(jnp.logical_not(keeps))
    def _():
        arrived(y_final.at[0], yf_recv.at[0])
        arrived(z_final.at[0], zf_recv.at[0])

    right = y_final[0]
    for step in range(1, NZ):
        arrived(y_final.at[step], yf_recv.at[step])
        right = right + y_final[step]
    left = z_final[0]
    for step in range(1, NY):
        arrived(z_final.at[step], zf_recv.at[step])
        left = left + z_final[step]
    out_ref[...] = jnp.concatenate([left, right], axis=1) * (1.0 / 65536.0)

    for copy in sends:
        copy.wait_send()
    for part in range(2):
        for_each_y(part, lambda copy: copy.wait_send())
        for_each_zf(part, lambda copy: copy.wait_send())

    @pl.when(keeps)
    def _():
        for part in range(2):
            for copy in yf_copies(part):
                copy.wait_send()


def body(design, filter_taps, segment, valid_flags, weights, block_ids):
    vmem = pl.BlockSpec(memory_space=pltpu.VMEM)
    dma = pltpu.SemaphoreType.DMA
    kinds = len(SOURCES)
    return pl.pallas_call(
        kernel,
        out_shape=jax.ShapeDtypeStruct((4, CB), F32),
        in_specs=[pl.BlockSpec(memory_space=pl.ANY)] * 6,
        out_specs=vmem,
        scratch_shapes=[
            pltpu.VMEM((EP, 2, CB), BF16),
            pltpu.VMEM((SEGS, 2, TAPS), BF16),
            pltpu.VMEM((1, EP), jnp.int32),
            pltpu.VMEM((1, EP), jnp.int32),
            pltpu.VMEM((2, EP), F32),
            pltpu.SMEM((BLOCKS,), jnp.int32),
            pltpu.VMEM((2, EP, CB), BF16),
            pltpu.VMEM((2, WINDOW, HALF), BF16),
            pltpu.VMEM((2, EP), F32),
            pltpu.VMEM((2, 2, EP), F32),
            pltpu.VMEM((2, 1, EP), jnp.int32),
            pltpu.VMEM((2, SPAN, WINDOW), BF16),
            pltpu.VMEM((NX, HALF, SPAN), BF16),
            pltpu.VMEM((NX, HALF, SPAN), BF16),
            pltpu.VMEM((2, 2, HALF, SPAN), BF16),
            pltpu.VMEM((NZ, BLOCKS, 8, HALF), F32),
            pltpu.VMEM((BLOCKS, NZ, 8, HALF), F32),
            pltpu.VMEM((kinds, BLOCKS, 8, HALF), F32),
            pltpu.VMEM((2, BLOCKS, 8, HALF), F32),
            pltpu.VMEM((2, BLOCKS, 8, HALF), F32),
            pltpu.VMEM((BLOCKS, 2, 4, HALF), F32),
            pltpu.VMEM((NY, 4, HALF), F32),
            pltpu.VMEM((NY, NZ, 8, HALF), F32),
            pltpu.VMEM((NZ, 2, 4, HALF), F32),
            pltpu.VMEM((NZ, 4, HALF), F32),
            dma((2, 2)),
            dma((2, 2)),
            dma((2, 2)),
            dma((2, 2)),
            dma((2,)),
            dma((2,)),
            dma((2, 2)),
            dma((2, 2)),
            dma((2, 6)),
            dma((2, 6)),
            dma((2,)),
            dma((2,)),
            dma((kinds, 2)),
            dma((kinds, 2)),
            dma((2, 2)),
            dma((2, 2)),
            dma((BLOCKS, 2)),
            dma((NY,)),
            dma((BLOCKS, 2)),
            dma((NY, 2)),
            dma((NZ, 2)),
            dma((NZ,)),
            pltpu.SemaphoreType.REGULAR((6,)),
            dma((6,)),
        ],
        compiler_params=pltpu.CompilerParams(collective_id=0, has_side_effects=True, vmem_limit_bytes=GRANT),
    )(design, filter_taps, segment.reshape(1, EP), valid_flags.reshape(1, EP), weights, block_ids)


def solution(mesh):
    return jax.shard_map(
        body,
        mesh=mesh,
        in_specs=(P("tm", None, "col"), P(), P("tm"), P("tm"), P(None, "tm"), P()),
        out_specs=P("tm", "col"),
        check_vma=False,
    )
```

```python
import jax
import jax.numpy as jnp
from jax import lax
from jax.experimental import pallas as pl
from jax.experimental.pallas import tpu as pltpu
from jax.sharding import PartitionSpec as P

MESH = pl.DeviceIdType.MESH
NY, NZ, NX = 8, 16, 4
CHIPS = NY * NZ
EP = 128
CB = 256
HALF = 128
TAPS = 512
SEGS = 256
BLOCKS = 4
SPAN = 2 * EP
WINDOW = TAPS + SPAN
GRANT = 54 * 1024 * 1024 - 96 * 1024
F32 = jnp.float32
BF16 = jnp.bfloat16

COLLECTOR = {8: 5, 7: 5, -7: -5, 6: 5, -6: -5, 4: 5, -4: -5, 3: 5, -3: -5, 2: 0, -2: 0, 1: 0, -1: 0}
SOURCES = list(COLLECTOR)


def kernel(
    design_in,
    taps_in,
    segment_in,
    valid_in,
    weight_in,
    ids_in,
    out_ref,
    design_ref,
    taps_ref,
    segment_ref,
    valid_ref,
    weight_ref,
    ids_ref,
    rows,
    window,
    side_mine,
    side_weight,
    side_segment,
    toeplitz,
    gathered_0,
    gathered_1,
    scaled,
    gram_z,
    gram_y,
    z_slots,
    middle,
    z_tops,
    total_z,
    z_final,
    y_slots,
    total_y,
    y_final,
    first_send,
    first_recv,
    last_send,
    last_recv,
    own_send,
    own_recv,
    side_send,
    side_recv,
    col_send,
    col_recv,
    q_send,
    q_recv,
    z_send,
    z_recv,
    top_send,
    top_recv,
    zf_send,
    zf_recv,
    y_send,
    y_recv,
    yf_send,
    yf_recv,
    token,
    load_sem,
):
    loads = [
        pltpu.make_async_copy(src, dst, load_sem.at[index])
        for index, (src, dst) in enumerate(
            (
                (design_in, design_ref),
                (segment_in, segment_ref),
                (valid_in, valid_ref),
                (weight_in, weight_ref),
                (taps_in, taps_ref),
                (ids_in, ids_ref),
            )
        )
    ]
    for load in loads:
        load.start()

    tm = lax.axis_index("tm")
    x = lax.axis_index("col")
    h = lax.rem(tm, 2)
    chip = tm // 2
    z = lax.rem(chip, NZ)
    y = chip // NZ
    other = 1 - h
    y_core = lax.rem(y, 2)
    keeps = h == y_core
    gathered = (gathered_0, gathered_1)

    def dev(chip_at, core, x_at=x):
        return {"tm": chip_at * 2 + core, "col": x_at}

    def along_z(offset, core=h):
        return dev(y * NZ + lax.rem(z + offset + NZ, NZ), core)

    def along_y(offset, core=h):
        return dev(lax.rem(y + offset + NY, NY) * NZ + z, core)

    def remote(src, dst, send_sem, recv_sem, device):
        return pltpu.make_async_remote_copy(
            src_ref=src, dst_ref=dst, send_sem=send_sem, recv_sem=recv_sem, device_id=device, device_id_type=MESH
        )

    pair = dev(chip, other)
    next_chip = lax.rem(chip + 1, CHIPS)
    prev_chip = lax.rem(chip + CHIPS - 1, CHIPS)
    x_up, x_down = lax.rem(x + 1, NX), lax.rem(x + NX - 1, NX)
    x_far = lax.rem(x + 2, NX)

    sends = []

    def start(copy):
        copy.start()
        sends.append(copy)

    def arrived(dst, recv_sem):
        remote(dst, dst, own_send.at[0], recv_sem, pair).wait_recv()

    def tell(which, devices):
        for device in devices:
            pl.semaphore_signal(token.at[which], inc=1, device_id=device, device_id_type=MESH)

    barrier = pltpu.get_barrier_semaphore()
    greeted = [
        pair,
        dev(prev_chip, 0),
        dev(prev_chip, 1),
        dev(next_chip, 0),
        dev(next_chip, 1),
        dev(chip, h, x_up),
        dev(chip, h, x_down),
        along_z(1),
        along_z(-1),
        along_y(1),
        along_y(-1),
    ]
    for device in greeted:
        pl.semaphore_signal(barrier, inc=1, device_id=device, device_id_type=MESH)
    loads[0].wait()
    rows[0] = design_ref[:, 0, :]
    pl.semaphore_wait(barrier, len(greeted))

    first_rows = pl.ds(pl.multiple_of(EP * h, EP), EP)
    own_rows = pl.ds(pl.multiple_of(SPAN + EP * h, EP), EP)
    last_rows = pl.ds(pl.multiple_of(2 * SPAN + EP * h, EP), EP)
    my_cols = pl.ds(pl.multiple_of(HALF * h, HALF), HALF)
    other_cols = pl.ds(pl.multiple_of(HALF * other, HALF), HALF)

    for load in loads[1:4]:
        load.wait()
    side_mine[...] = weight_ref[...] * valid_ref[...].astype(F32)
    for core in range(2):
        start(
            remote(
                segment_ref, side_segment.at[h], side_send.at[0, core], side_recv.at[0, h], dev(prev_chip, core)
            )
        )
    for k in range(2):
        if k == 1:
            rows[1] = design_ref[:, 1, :]
        for core in range(2):
            half = rows.at[k, :, pl.ds(HALF * core, HALF)]
            start(
                remote(
                    half, window.at[k, last_rows, :], last_send.at[k, core], last_recv.at[k, h], dev(prev_chip, core)
                )
            )
            start(
                remote(
                    half, window.at[k, first_rows, :], first_send.at[k, core], first_recv.at[k, h], dev(next_chip, core)
                )
            )
        start(
            remote(
                rows.at[k, :, other_cols], window.at[k, own_rows, :], own_send.at[k], own_recv.at[k], pair
            )
        )
    for core in range(2):
        start(
            remote(side_mine, side_weight.at[h], side_send.at[1, core], side_recv.at[1, h], dev(prev_chip, core))
        )
    tell(0, [along_z(1), along_z(-1)])
    tell(1, [along_y(1), along_y(-1)])
    for k in range(2):
        window[k, own_rows, :] = rows[k, :, my_cols]

    flip = (
        lax.broadcasted_iota(jnp.int32, (TAPS, TAPS), 0) + lax.broadcasted_iota(jnp.int32, (TAPS, TAPS), 1)
        == TAPS - 1
    ).astype(F32).astype(BF16)
    first_row = jnp.where(chip == CHIPS - 1, TAPS, jnp.where(chip == 0, SPAN, 0))
    lane = lax.broadcasted_iota(jnp.int32, (SPAN, WINDOW), 1)
    for core in range(2):
        arrived(side_segment.at[core], side_recv.at[0, core])
    segments = jnp.concatenate([side_segment[0], side_segment[1]], axis=1)
    selector = (lax.broadcasted_iota(jnp.int32, (SEGS, SPAN), 0) == segments).astype(F32).astype(BF16)

    def build(k):
        tap_rows = lax.dot_general(
            selector, taps_ref[:, k, :], (((0,), (0,)), ((), ())), preferred_element_type=F32
        ).astype(BF16)
        flipped = jnp.dot(tap_rows, flip, preferred_element_type=F32)
        wide = jnp.concatenate([flipped, jnp.zeros((SPAN, SPAN), F32)], axis=1)
        skewed = pltpu.roll(wide, 1, 1, stride=1, stride_axis=0)
        toeplitz[k] = jnp.where(lane >= first_row, skewed, 0.0).astype(BF16)

    loads[4].wait()
    loads[5].wait()
    build(0)
    pl.semaphore_wait(token.at[0], 2)
    pl.semaphore_wait(token.at[1], 2)
    tell(2, [along_z(2), along_z(-2)])
    tell(3, [along_y(2), along_y(-2)])

    def piece(k, at, side):
        return gathered[k].at[at, pl.ds(side * HALF // 2, HALF // 2)]

    def send_piece(k, at, side, which, x_to):
        start(remote(piece(k, at, side), piece(k, at, side), col_send.at[k, which], col_recv.at[k, which], dev(chip, h, x_to)))

    def part(k, at):
        span = pl.ds(SPAN * at, SPAN)
        return jnp.dot(toeplitz[k, :, span], window[k, span, :], preferred_element_type=F32)

    def filter_and_send(k):
        arrived(window.at[k, pl.ds(pl.multiple_of(SPAN + EP * other, EP), EP), :], own_recv.at[k])
        added = part(k, 1)
        for core in range(2):
            arrived(window.at[k, pl.ds(EP * core, EP), :], first_recv.at[k, core])
        added = added + part(k, 0)
        for core in range(2):
            arrived(window.at[k, pl.ds(2 * SPAN + EP * core, EP), :], last_recv.at[k, core])
        added = added + part(k, 2)
        gathered[k][x] = added.T.astype(BF16)
        send_piece(k, x, 0, 0, x_up)
        send_piece(k, x, 1, 1, x_down)
        send_piece(k, x, 1, 2, x_up)
        send_piece(k, x, 0, 3, x_down)

    def relay(k):
        arrived(piece(k, x_down, 0), col_recv.at[k, 0])
        send_piece(k, x_down, 0, 4, x_up)
        arrived(piece(k, x_up, 1), col_recv.at[k, 1])
        send_piece(k, x_up, 1, 5, x_down)

    def block_of(wanted):
        found = jnp.int32(0)
        for d in range(1, BLOCKS):
            found = jnp.where(ids_ref[d] == wanted, d, found)
        return found

    def scale(k):
        arrived(piece(k, x_down, 1), col_recv.at[k, 2])
        arrived(piece(k, x_up, 0), col_recv.at[k, 3])
        arrived(piece(k, x_far, 0), col_recv.at[k, 4])
        arrived(piece(k, x_far, 1), col_recv.at[k, 5])
        row_weight = jnp.concatenate([side_weight[0, k : k + 1], side_weight[1, k : k + 1]], axis=1)
        scaled[k, h] = (gathered[k][block_of(x)].astype(F32) * row_weight).astype(BF16)
        start(remote(scaled.at[k, h], scaled.at[k, h], q_send.at[k], q_recv.at[k], pair))

    first_step = jnp.where(keeps, NY // 2, NY // 2 - 1)

    def place(b):
        return lax.rem(2 * b + h - y - first_step + 2 * NY, NY) // 2

    def y_copy(at, part):
        step = lax.rem(2 * at + first_step, NY)
        span = pl.ds(part * NZ // 2, NZ // 2)
        return remote(
            gram_y.at[at, span],
            y_slots.at[step, span],
            y_send.at[at, part],
            y_recv.at[step, part],
            along_y(2 * at + first_step),
        )

    def for_each_y(part, act):
        for at in range(BLOCKS):
            if at == 2:

                @pl.when(jnp.logical_not(keeps))
                def _():
                    act(y_copy(at, part))

            else:
                act(y_copy(at, part))

    def multiply(k):
        arrived(scaled.at[k, other], q_recv.at[k])
        right = scaled[k].reshape(CB, SPAN)
        for b in range(BLOCKS):
            product = lax.dot_general(
                gathered[k][block_of(b)], right, (((1,), (1,)), ((), ())), preferred_element_type=F32
            ).reshape(NZ, 8, CB)
            at = place(b)
            if k == 0:
                gram_z[:, at] = product[:, :, :HALF]
            else:
                gram_z[:, at] += product[:, :, :HALF]
            for row in range(NZ):
                turned = lax.rem(row - z - 4 + 2 * NZ, NZ)
                if k == 0:
                    gram_y[at, turned] = product[row, :, HALF:]
                else:
                    gram_y[at, turned] += product[row, :, HALF:]

    filter_and_send(0)
    build(1)
    pl.semaphore_wait(token.at[2], 2)
    pl.semaphore_wait(token.at[3], 2)
    tell(4, [along_z(4), along_z(-4)])
    filter_and_send(1)
    relay(0)
    pl.semaphore_wait(token.at[4], 2)
    tell(5, [pair])
    for core in range(2):
        arrived(side_weight.at[core], side_recv.at[1, core])
    relay(1)
    scale(0)
    scale(1)
    multiply(0)
    pl.semaphore_wait(token.at[5], 1)
    multiply(1)

    def z_pair(part):
        return pl.ds(2 * part, 2)

    def send_z(part, near):
        for index, s in enumerate(SOURCES):
            if (COLLECTOR[s] == 0) == near:
                start(
                    remote(
                        gram_z.at[lax.rem(z - s + NZ, NZ), z_pair(part)],
                        z_slots.at[index, z_pair(part)],
                        z_send.at[index, part],
                        z_recv.at[index, part],
                        along_z(COLLECTOR[s] - s),
                    )
                )

    send_z(0, False)
    for_each_y(0, lambda copy: copy.start())
    send_z(1, False)
    for_each_y(1, lambda copy: copy.start())
    send_z(0, True)
    send_z(1, True)

    def collect(into, own, part):
        added = gram_z[own, z_pair(part)]
        for index, s in enumerate(SOURCES):
            if COLLECTOR[s] == into:
                arrived(z_slots.at[index, z_pair(part)], z_recv.at[index, part])
                added = added + z_slots[index, z_pair(part)]
        return added

    for part in range(2):
        for index, to in enumerate((-5, 5)):
            middle[index, z_pair(part)] = collect(to, lax.rem(z - to + NZ, NZ), part)
            start(
                remote(
                    middle.at[index, z_pair(part)],
                    z_tops.at[index, z_pair(part)],
                    top_send.at[index, part],
                    top_recv.at[index, part],
                    along_z(-to),
                )
            )

    def yf_copies(part):
        out = []
        for step in ((8, 7, 9, 6, 10, 5, 11, 4), (12, 3, 13, 2, 14, 1, 15, 0))[part]:
            for core in range(2):
                if step:
                    out.append(
                        remote(
                            total_y.at[(step - 4) % NZ, core],
                            y_final.at[step],
                            yf_send.at[step, core],
                            yf_recv.at[step],
                            along_z(step, core),
                        )
                    )
        if part == 1:
            out.append(remote(total_y.at[NZ - 4, other], y_final.at[0], yf_send.at[0, 0], yf_recv.at[0], pair))
        return out

    @pl.when(keeps)
    def _():
        for part in range(2):
            span = pl.ds(part * NZ // 2, NZ // 2)
            added = gram_y[2, span]
            for step in range(1, NY):
                arrived(y_slots.at[step, span], y_recv.at[step, part])
                added = added + y_slots[step, span]
            total_y[span, 0] = added[:, :4]
            total_y[span, 1] = added[:, 4:]
            for copy in yf_copies(part):
                copy.start()
        y_final[0] = total_y[NZ - 4, h]

    def zf_copy(at, core):
        step = lax.rem(2 * at + first_step, NY)
        return remote(
            total_z.at[at, core],
            z_final.at[step],
            zf_send.at[at, core],
            zf_recv.at[step],
            along_y(2 * at + first_step, core),
        )

    def for_each_zf(part, act):
        for at in (2 * part, 2 * part + 1):
            for core in range(2):
                if at == 2:

                    @pl.when(jnp.logical_not(jnp.logical_and(keeps, h == core)))
                    def _():
                        act(zf_copy(at, core))

                else:
                    act(zf_copy(at, core))

    for part in range(2):
        summed = collect(0, z, part)
        for index in range(2):
            arrived(z_tops.at[index, z_pair(part)], top_recv.at[index, part])
            summed = summed + z_tops[index, z_pair(part)]
        total_z[z_pair(part), 0] = summed[:, :4]
        total_z[z_pair(part), 1] = summed[:, 4:]
        for_each_zf(part, lambda copy: copy.start())

    @pl.when(keeps)
    def _():
        z_final[0] = total_z[2, h]

    @pl.when(jnp.logical_not(keeps))
    def _():
        arrived(y_final.at[0], yf_recv.at[0])
        arrived(z_final.at[0], zf_recv.at[0])

    right = y_final[0]
    for step in range(1, NZ):
        arrived(y_final.at[step], yf_recv.at[step])
        right = right + y_final[step]
    left = z_final[0]
    for step in range(1, NY):
        arrived(z_final.at[step], zf_recv.at[step])
        left = left + z_final[step]
    out_ref[...] = jnp.concatenate([left, right], axis=1) * (1.0 / 65536.0)

    for copy in sends:
        copy.wait_send()
    for part in range(2):
        for_each_y(part, lambda copy: copy.wait_send())
        for_each_zf(part, lambda copy: copy.wait_send())

    @pl.when(keeps)
    def _():
        for part in range(2):
            for copy in yf_copies(part):
                copy.wait_send()


def body(design, filter_taps, segment, valid_flags, weights, block_ids):
    vmem = pl.BlockSpec(memory_space=pltpu.VMEM)
    dma = pltpu.SemaphoreType.DMA
    kinds = len(SOURCES)
    return pl.pallas_call(
        kernel,
        out_shape=jax.ShapeDtypeStruct((4, CB), F32),
        in_specs=[pl.BlockSpec(memory_space=pl.ANY)] * 6,
        out_specs=vmem,
        scratch_shapes=[
            pltpu.VMEM((EP, 2, CB), BF16),
            pltpu.VMEM((SEGS, 2, TAPS), BF16),
            pltpu.VMEM((1, EP), jnp.int32),
            pltpu.VMEM((1, EP), jnp.int32),
            pltpu.VMEM((2, EP), F32),
            pltpu.SMEM((BLOCKS,), jnp.int32),
            pltpu.VMEM((2, EP, CB), BF16),
            pltpu.VMEM((2, WINDOW, HALF), BF16),
            pltpu.VMEM((2, EP), F32),
            pltpu.VMEM((2, 2, EP), F32),
            pltpu.VMEM((2, 1, EP), jnp.int32),
            pltpu.VMEM((2, SPAN, WINDOW), BF16),
            pltpu.VMEM((NX, HALF, SPAN), BF16),
            pltpu.VMEM((NX, HALF, SPAN), BF16),
            pltpu.VMEM((2, 2, HALF, SPAN), BF16),
            pltpu.VMEM((NZ, BLOCKS, 8, HALF), F32),
            pltpu.VMEM((BLOCKS, NZ, 8, HALF), F32),
            pltpu.VMEM((kinds, BLOCKS, 8, HALF), F32),
            pltpu.VMEM((2, BLOCKS, 8, HALF), F32),
            pltpu.VMEM((2, BLOCKS, 8, HALF), F32),
            pltpu.VMEM((BLOCKS, 2, 4, HALF), F32),
            pltpu.VMEM((NY, 4, HALF), F32),
            pltpu.VMEM((NY, NZ, 8, HALF), F32),
            pltpu.VMEM((NZ, 2, 4, HALF), F32),
            pltpu.VMEM((NZ, 4, HALF), F32),
            dma((2, 2)),
            dma((2, 2)),
            dma((2, 2)),
            dma((2, 2)),
            dma((2,)),
            dma((2,)),
            dma((2, 2)),
            dma((2, 2)),
            dma((2, 6)),
            dma((2, 6)),
            dma((2,)),
            dma((2,)),
            dma((kinds, 2)),
            dma((kinds, 2)),
            dma((2, 2)),
            dma((2, 2)),
            dma((BLOCKS, 2)),
            dma((NY,)),
            dma((BLOCKS, 2)),
            dma((NY, 2)),
            dma((NZ, 2)),
            dma((NZ,)),
            pltpu.SemaphoreType.REGULAR((6,)),
            dma((6,)),
        ],
        compiler_params=pltpu.CompilerParams(collective_id=0, has_side_effects=True, vmem_limit_bytes=GRANT),
    )(design, filter_taps, segment.reshape(1, EP), valid_flags.reshape(1, EP), weights, block_ids)


def solution(mesh):
    return jax.shard_map(
        body,
        mesh=mesh,
        in_specs=(P("tm", None, "col"), P(), P("tm"), P("tm"), P(None, "tm"), P()),
        out_specs=P("tm", "col"),
        check_vma=False,
    )
```

```python
import jax
import jax.numpy as jnp
from jax import lax
from jax.experimental import pallas as pl
from jax.experimental.pallas import tpu as pltpu
from jax.sharding import PartitionSpec as P

MESH = pl.DeviceIdType.MESH
NY, NZ, NX = 8, 16, 4
CHIPS = NY * NZ
EP = 128
CB = 256
HALF = 128
TAPS = 512
SEGS = 256
BLOCKS = 4
SPAN = 2 * EP
WINDOW = TAPS + SPAN
GRANT = 54 * 1024 * 1024 - 96 * 1024
F32 = jnp.float32
BF16 = jnp.bfloat16

COLLECTOR = {8: 5, 7: 5, -7: -5, 6: 5, -6: -5, 4: 5, -4: -5, 3: 5, -3: -5, 2: 0, -2: 0, 1: 0, -1: 0}
SOURCES = list(COLLECTOR)


def kernel(
    design_in,
    taps_in,
    segment_in,
    valid_in,
    weight_in,
    ids_in,
    out_ref,
    design_ref,
    taps_ref,
    segment_ref,
    valid_ref,
    weight_ref,
    ids_ref,
    rows,
    window,
    side_mine,
    side_weight,
    side_segment,
    flipped_taps,
    toeplitz,
    gathered_0,
    gathered_1,
    scaled,
    gram_z,
    gram_y,
    z_slots,
    middle,
    z_tops,
    total_z,
    z_final,
    y_slots,
    total_y,
    y_final,
    first_send,
    first_recv,
    last_send,
    last_recv,
    own_send,
    own_recv,
    side_send,
    side_recv,
    col_send,
    col_recv,
    q_send,
    q_recv,
    z_send,
    z_recv,
    top_send,
    top_recv,
    zf_send,
    zf_recv,
    y_send,
    y_recv,
    yf_send,
    yf_recv,
    token,
    load_sem,
):
    loads = [
        pltpu.make_async_copy(src, dst, load_sem.at[index])
        for index, (src, dst) in enumerate(
            (
                (design_in, design_ref),
                (segment_in, segment_ref),
                (valid_in, valid_ref),
                (weight_in, weight_ref),
                (taps_in, taps_ref),
                (ids_in, ids_ref),
            )
        )
    ]
    for load in loads:
        load.start()

    tm = lax.axis_index("tm")
    x = lax.axis_index("col")
    h = lax.rem(tm, 2)
    chip = tm // 2
    z = lax.rem(chip, NZ)
    y = chip // NZ
    other = 1 - h
    y_core = lax.rem(y, 2)
    keeps = h == y_core
    gathered = (gathered_0, gathered_1)

    def dev(chip_at, core, x_at=x):
        return {"tm": chip_at * 2 + core, "col": x_at}

    def along_z(offset, core=h):
        return dev(y * NZ + lax.rem(z + offset + NZ, NZ), core)

    def along_y(offset, core=h):
        return dev(lax.rem(y + offset + NY, NY) * NZ + z, core)

    def remote(src, dst, send_sem, recv_sem, device):
        return pltpu.make_async_remote_copy(
            src_ref=src, dst_ref=dst, send_sem=send_sem, recv_sem=recv_sem, device_id=device, device_id_type=MESH
        )

    pair = dev(chip, other)
    next_chip = lax.rem(chip + 1, CHIPS)
    prev_chip = lax.rem(chip + CHIPS - 1, CHIPS)
    x_up, x_down = lax.rem(x + 1, NX), lax.rem(x + NX - 1, NX)
    x_far = lax.rem(x + 2, NX)

    sends = []

    def start(copy):
        copy.start()
        sends.append(copy)

    def arrived(dst, recv_sem):
        remote(dst, dst, own_send.at[0], recv_sem, pair).wait_recv()

    def tell(which, devices):
        for device in devices:
            pl.semaphore_signal(token.at[which], inc=1, device_id=device, device_id_type=MESH)

    barrier = pltpu.get_barrier_semaphore()
    greeted = [
        pair,
        dev(prev_chip, 0),
        dev(prev_chip, 1),
        dev(next_chip, 0),
        dev(next_chip, 1),
        dev(chip, h, x_up),
        dev(chip, h, x_down),
        along_z(1),
        along_z(-1),
        along_y(1),
        along_y(-1),
    ]
    for device in greeted:
        pl.semaphore_signal(barrier, inc=1, device_id=device, device_id_type=MESH)
    loads[0].wait()
    rows[0] = design_ref[:, 0, :]
    pl.semaphore_wait(barrier, len(greeted))

    first_rows = pl.ds(pl.multiple_of(EP * h, EP), EP)
    own_rows = pl.ds(pl.multiple_of(SPAN + EP * h, EP), EP)
    last_rows = pl.ds(pl.multiple_of(2 * SPAN + EP * h, EP), EP)
    my_cols = pl.ds(pl.multiple_of(HALF * h, HALF), HALF)
    other_cols = pl.ds(pl.multiple_of(HALF * other, HALF), HALF)

    for load in loads[1:4]:
        load.wait()
    side_mine[...] = weight_ref[...] * valid_ref[...].astype(F32)
    for core in range(2):
        start(
            remote(
                segment_ref, side_segment.at[h], side_send.at[0, core], side_recv.at[0, h], dev(prev_chip, core)
            )
        )
    for k in range(2):
        if k == 1:
            rows[1] = design_ref[:, 1, :]
        for core in range(2):
            half = rows.at[k, :, pl.ds(HALF * core, HALF)]
            start(
                remote(
                    half, window.at[k, last_rows, :], last_send.at[k, core], last_recv.at[k, h], dev(prev_chip, core)
                )
            )
            start(
                remote(
                    half, window.at[k, first_rows, :], first_send.at[k, core], first_recv.at[k, h], dev(next_chip, core)
                )
            )
        start(
            remote(
                rows.at[k, :, other_cols], window.at[k, own_rows, :], own_send.at[k], own_recv.at[k], pair
            )
        )
    for core in range(2):
        start(
            remote(side_mine, side_weight.at[h], side_send.at[1, core], side_recv.at[1, h], dev(prev_chip, core))
        )
    tell(0, [along_z(1), along_z(-1)])
    tell(1, [along_y(1), along_y(-1)])
    for k in range(2):
        window[k, own_rows, :] = rows[k, :, my_cols]

    flip = (
        lax.broadcasted_iota(jnp.int32, (TAPS, TAPS), 0) + lax.broadcasted_iota(jnp.int32, (TAPS, TAPS), 1)
        == TAPS - 1
    ).astype(F32).astype(BF16)
    first_row = jnp.where(chip == CHIPS - 1, TAPS, jnp.where(chip == 0, SPAN, 0))
    lane = lax.broadcasted_iota(jnp.int32, (SPAN, WINDOW), 1)
    loads[4].wait()
    for k in range(2):
        flipped_taps[k] = jnp.dot(taps_ref[:, k, :], flip, preferred_element_type=F32).astype(BF16)
    for core in range(2):
        arrived(side_segment.at[core], side_recv.at[0, core])
    segments = jnp.concatenate([side_segment[0], side_segment[1]], axis=1)
    selector = (lax.broadcasted_iota(jnp.int32, (SEGS, SPAN), 0) == segments).astype(F32).astype(BF16)

    def build(k):
        flipped = lax.dot_general(
            selector, flipped_taps[k], (((0,), (0,)), ((), ())), preferred_element_type=F32
        )
        wide = jnp.concatenate([flipped, jnp.zeros((SPAN, SPAN), F32)], axis=1)
        skewed = pltpu.roll(wide, 1, 1, stride=1, stride_axis=0)
        toeplitz[k] = jnp.where(lane >= first_row, skewed, 0.0).astype(BF16)

    loads[5].wait()
    build(0)
    pl.semaphore_wait(token.at[0], 2)
    pl.semaphore_wait(token.at[1], 2)
    tell(2, [along_z(2), along_z(-2)])
    tell(3, [along_y(2), along_y(-2)])

    def piece(k, at, side):
        return gathered[k].at[at, pl.ds(side * HALF // 2, HALF // 2)]

    def send_piece(k, at, side, which, x_to):
        start(remote(piece(k, at, side), piece(k, at, side), col_send.at[k, which], col_recv.at[k, which], dev(chip, h, x_to)))

    def part(k, at):
        span = pl.ds(SPAN * at, SPAN)
        return jnp.dot(toeplitz[k, :, span], window[k, span, :], preferred_element_type=F32)

    def filter_and_send(k):
        arrived(window.at[k, pl.ds(pl.multiple_of(SPAN + EP * other, EP), EP), :], own_recv.at[k])
        added = part(k, 1)
        for core in range(2):
            arrived(window.at[k, pl.ds(EP * core, EP), :], first_recv.at[k, core])
        added = added + part(k, 0)
        for core in range(2):
            arrived(window.at[k, pl.ds(2 * SPAN + EP * core, EP), :], last_recv.at[k, core])
        added = added + part(k, 2)
        gathered[k][x] = added.T.astype(BF16)
        send_piece(k, x, 0, 0, x_up)
        send_piece(k, x, 1, 1, x_down)
        send_piece(k, x, 1, 2, x_up)
        send_piece(k, x, 0, 3, x_down)

    def relay(k):
        arrived(piece(k, x_down, 0), col_recv.at[k, 0])
        send_piece(k, x_down, 0, 4, x_up)
        arrived(piece(k, x_up, 1), col_recv.at[k, 1])
        send_piece(k, x_up, 1, 5, x_down)

    def block_of(wanted):
        found = jnp.int32(0)
        for d in range(1, BLOCKS):
            found = jnp.where(ids_ref[d] == wanted, d, found)
        return found

    def scale(k):
        arrived(piece(k, x_down, 1), col_recv.at[k, 2])
        arrived(piece(k, x_up, 0), col_recv.at[k, 3])
        arrived(piece(k, x_far, 0), col_recv.at[k, 4])
        arrived(piece(k, x_far, 1), col_recv.at[k, 5])
        row_weight = jnp.concatenate([side_weight[0, k : k + 1], side_weight[1, k : k + 1]], axis=1)
        scaled[k, h] = (gathered[k][block_of(x)].astype(F32) * row_weight).astype(BF16)
        start(remote(scaled.at[k, h], scaled.at[k, h], q_send.at[k], q_recv.at[k], pair))

    first_step = jnp.where(keeps, NY // 2, NY // 2 - 1)

    def place(b):
        return lax.rem(2 * b + h - y - first_step + 2 * NY, NY) // 2

    def y_copy(at, part):
        step = lax.rem(2 * at + first_step, NY)
        span = pl.ds(part * NZ // 2, NZ // 2)
        return remote(
            gram_y.at[at, span],
            y_slots.at[step, span],
            y_send.at[at, part],
            y_recv.at[step, part],
            along_y(2 * at + first_step),
        )

    def for_each_y(part, act):
        for at in range(BLOCKS):
            if at == 2:

                @pl.when(jnp.logical_not(keeps))
                def _():
                    act(y_copy(at, part))

            else:
                act(y_copy(at, part))

    def multiply(k):
        arrived(scaled.at[k, other], q_recv.at[k])
        right = scaled[k].reshape(CB, SPAN)
        for b in range(BLOCKS):
            product = lax.dot_general(
                gathered[k][block_of(b)], right, (((1,), (1,)), ((), ())), preferred_element_type=F32
            ).reshape(NZ, 8, CB)
            at = place(b)
            if k == 0:
                gram_z[:, at] = product[:, :, :HALF]
            else:
                gram_z[:, at] += product[:, :, :HALF]
            for row in range(NZ):
                turned = lax.rem(row - z - 4 + 2 * NZ, NZ)
                if k == 0:
                    gram_y[at, turned] = product[row, :, HALF:]
                else:
                    gram_y[at, turned] += product[row, :, HALF:]

    filter_and_send(0)
    build(1)
    pl.semaphore_wait(token.at[2], 2)
    pl.semaphore_wait(token.at[3], 2)
    tell(4, [along_z(4), along_z(-4)])
    filter_and_send(1)
    relay(0)
    pl.semaphore_wait(token.at[4], 2)
    tell(5, [pair])
    for core in range(2):
        arrived(side_weight.at[core], side_recv.at[1, core])
    relay(1)
    scale(0)
    scale(1)
    multiply(0)
    pl.semaphore_wait(token.at[5], 1)
    multiply(1)

    def z_pair(part):
        return pl.ds(2 * part, 2)

    def send_z(part, near):
        for index, s in enumerate(SOURCES):
            if (COLLECTOR[s] == 0) == near:
                start(
                    remote(
                        gram_z.at[lax.rem(z - s + NZ, NZ), z_pair(part)],
                        z_slots.at[index, z_pair(part)],
                        z_send.at[index, part],
                        z_recv.at[index, part],
                        along_z(COLLECTOR[s] - s),
                    )
                )

    send_z(0, False)
    for_each_y(0, lambda copy: copy.start())
    send_z(1, False)
    for_each_y(1, lambda copy: copy.start())
    send_z(0, True)
    send_z(1, True)

    def collect(into, own, part):
        added = gram_z[own, z_pair(part)]
        for index, s in enumerate(SOURCES):
            if COLLECTOR[s] == into:
                arrived(z_slots.at[index, z_pair(part)], z_recv.at[index, part])
                added = added + z_slots[index, z_pair(part)]
        return added

    for part in range(2):
        for index, to in enumerate((-5, 5)):
            middle[index, z_pair(part)] = collect(to, lax.rem(z - to + NZ, NZ), part)
            start(
                remote(
                    middle.at[index, z_pair(part)],
                    z_tops.at[index, z_pair(part)],
                    top_send.at[index, part],
                    top_recv.at[index, part],
                    along_z(-to),
                )
            )

    def yf_copies(part):
        out = []
        for step in ((8, 7, 9, 6, 10, 5, 11, 4), (12, 3, 13, 2, 14, 1, 15, 0))[part]:
            for core in range(2):
                if step:
                    out.append(
                        remote(
                            total_y.at[(step - 4) % NZ, core],
                            y_final.at[step],
                            yf_send.at[step, core],
                            yf_recv.at[step],
                            along_z(step, core),
                        )
                    )
        if part == 1:
            out.append(remote(total_y.at[NZ - 4, other], y_final.at[0], yf_send.at[0, 0], yf_recv.at[0], pair))
        return out

    @pl.when(keeps)
    def _():
        for part in range(2):
            span = pl.ds(part * NZ // 2, NZ // 2)
            added = gram_y[2, span]
            for step in range(1, NY):
                arrived(y_slots.at[step, span], y_recv.at[step, part])
                added = added + y_slots[step, span]
            total_y[span, 0] = added[:, :4]
            total_y[span, 1] = added[:, 4:]
            for copy in yf_copies(part):
                copy.start()
        y_final[0] = total_y[NZ - 4, h]

    def zf_copy(at, core):
        step = lax.rem(2 * at + first_step, NY)
        return remote(
            total_z.at[at, core],
            z_final.at[step],
            zf_send.at[at, core],
            zf_recv.at[step],
            along_y(2 * at + first_step, core),
        )

    def for_each_zf(part, act):
        for at in (2 * part, 2 * part + 1):
            for core in range(2):
                if at == 2:

                    @pl.when(jnp.logical_not(jnp.logical_and(keeps, h == core)))
                    def _():
                        act(zf_copy(at, core))

                else:
                    act(zf_copy(at, core))

    for part in range(2):
        summed = collect(0, z, part)
        for index in range(2):
            arrived(z_tops.at[index, z_pair(part)], top_recv.at[index, part])
            summed = summed + z_tops[index, z_pair(part)]
        total_z[z_pair(part), 0] = summed[:, :4]
        total_z[z_pair(part), 1] = summed[:, 4:]
        for_each_zf(part, lambda copy: copy.start())

    @pl.when(keeps)
    def _():
        z_final[0] = total_z[2, h]

    @pl.when(jnp.logical_not(keeps))
    def _():
        arrived(y_final.at[0], yf_recv.at[0])
        arrived(z_final.at[0], zf_recv.at[0])

    right = y_final[0]
    for step in range(1, NZ):
        arrived(y_final.at[step], yf_recv.at[step])
        right = right + y_final[step]
    left = z_final[0]
    for step in range(1, NY):
        arrived(z_final.at[step], zf_recv.at[step])
        left = left + z_final[step]
    out_ref[...] = jnp.concatenate([left, right], axis=1) * (1.0 / 65536.0)

    for copy in sends:
        copy.wait_send()
    for part in range(2):
        for_each_y(part, lambda copy: copy.wait_send())
        for_each_zf(part, lambda copy: copy.wait_send())

    @pl.when(keeps)
    def _():
        for part in range(2):
            for copy in yf_copies(part):
                copy.wait_send()


def body(design, filter_taps, segment, valid_flags, weights, block_ids):
    vmem = pl.BlockSpec(memory_space=pltpu.VMEM)
    dma = pltpu.SemaphoreType.DMA
    kinds = len(SOURCES)
    return pl.pallas_call(
        kernel,
        out_shape=jax.ShapeDtypeStruct((4, CB), F32),
        in_specs=[pl.BlockSpec(memory_space=pl.ANY)] * 6,
        out_specs=vmem,
        scratch_shapes=[
            pltpu.VMEM((EP, 2, CB), BF16),
            pltpu.VMEM((SEGS, 2, TAPS), BF16),
            pltpu.VMEM((1, EP), jnp.int32),
            pltpu.VMEM((1, EP), jnp.int32),
            pltpu.VMEM((2, EP), F32),
            pltpu.SMEM((BLOCKS,), jnp.int32),
            pltpu.VMEM((2, EP, CB), BF16),
            pltpu.VMEM((2, WINDOW, HALF), BF16),
            pltpu.VMEM((2, EP), F32),
            pltpu.VMEM((2, 2, EP), F32),
            pltpu.VMEM((2, 1, EP), jnp.int32),
            pltpu.VMEM((2, SEGS, TAPS), BF16),
            pltpu.VMEM((2, SPAN, WINDOW), BF16),
            pltpu.VMEM((NX, HALF, SPAN), BF16),
            pltpu.VMEM((NX, HALF, SPAN), BF16),
            pltpu.VMEM((2, 2, HALF, SPAN), BF16),
            pltpu.VMEM((NZ, BLOCKS, 8, HALF), F32),
            pltpu.VMEM((BLOCKS, NZ, 8, HALF), F32),
            pltpu.VMEM((kinds, BLOCKS, 8, HALF), F32),
            pltpu.VMEM((2, BLOCKS, 8, HALF), F32),
            pltpu.VMEM((2, BLOCKS, 8, HALF), F32),
            pltpu.VMEM((BLOCKS, 2, 4, HALF), F32),
            pltpu.VMEM((NY, 4, HALF), F32),
            pltpu.VMEM((NY, NZ, 8, HALF), F32),
            pltpu.VMEM((NZ, 2, 4, HALF), F32),
            pltpu.VMEM((NZ, 4, HALF), F32),
            dma((2, 2)),
            dma((2, 2)),
            dma((2, 2)),
            dma((2, 2)),
            dma((2,)),
            dma((2,)),
            dma((2, 2)),
            dma((2, 2)),
            dma((2, 6)),
            dma((2, 6)),
            dma((2,)),
            dma((2,)),
            dma((kinds, 2)),
            dma((kinds, 2)),
            dma((2, 2)),
            dma((2, 2)),
            dma((BLOCKS, 2)),
            dma((NY,)),
            dma((BLOCKS, 2)),
            dma((NY, 2)),
            dma((NZ, 2)),
            dma((NZ,)),
            pltpu.SemaphoreType.REGULAR((6,)),
            dma((6,)),
        ],
        compiler_params=pltpu.CompilerParams(collective_id=0, has_side_effects=True, vmem_limit_bytes=GRANT),
    )(design, filter_taps, segment.reshape(1, EP), valid_flags.reshape(1, EP), weights, block_ids)


def solution(mesh):
    return jax.shard_map(
        body,
        mesh=mesh,
        in_specs=(P("tm", None, "col"), P(), P("tm"), P("tm"), P(None, "tm"), P()),
        out_specs=P("tm", "col"),
        check_vma=False,
    )
```
